256 devices in a mesh: dp: 32 (over y, x, core), tensor: 8 (over z).
Axes of the slice: x: 4, y: 4, z: 8, core: 2. Of those that a mesh axis runs over, the one named last changes fastest.
Arguments:
- rank_query: bfloat16 [256, 32, 5120], P('dp', None, 'tensor'), may hold values from -4.5 to 4.5
- rank_key: bfloat16 [256, 32, 5120], P('dp', None, 'tensor'), may hold values from -4.5 to 4.5
- rank_value: bfloat16 [256, 32, 5120], P('dp', None, 'tensor'), may hold values from -6 to 6
- rank_resid: bfloat16 [256, 32, 5120], P(('dp', 'tensor')), may hold values from -4 to 4
- out_weight: bfloat16 [5120, 5120], P('tensor', 'dp'), may hold values from -0.25 to 0.25
- rank_gain: bfloat16 [5120], replicated, may hold values from 0.099609375 to 1.8984375
- score_weight: bfloat16 [5120], replicated, may hold values from -0.078125 to 0.078125
- pair_index: int32 [256, 3], P(('dp', 'tensor')), may hold values from 0 to 31, as said below
- cand_rank: int32 [1024, 8], P('dp'), may hold values from 0 to 7, each once within a row
- cand_len: int32 [1024, 8], P('dp'), may hold values from 1 to 8, 39 in all within a row
- blend_owner: int32 [32, 32], P('dp'), may hold values from 0 to 31, each once within a row
- blend_rows: bfloat16 [1024, 8, 8, 4096], P('dp', None, None, 'tensor'), may hold values from -6 to 6
- blend_gain: bfloat16 [4096], replicated, may hold values from 0.099609375 to 1.8984375
- blend_weight: bfloat16 [4096, 3, 2048], P('dp', None, 'tensor'), may hold values from -0.09375 to 0.09375
Outputs:
- rank_hidden: bfloat16 [256, 32, 5120], P(('dp', 'tensor'))
- cand_score: float32 [1024, 8], P('dp')
- blended_qkv: bfloat16 [1024, 24, 3, 2048], P('dp', None, None, 'tensor')
The draws below stay inside these ranges and needn't reach their ends.
Inputs may be any that keep to these rules, and one draw needn't show every extreme that they name: `pair_index`: column 0 is a prompt of the pair's own group of 32 prompts (pair p belongs to group p // 8); columns 1 and 2 are two different candidates of that prompt. `cand_rank`: each row gives every rank once. `blend_owner`: each row names every group once.
All inputs are finite; a program needn't handle non-finite values.
Results may differ from the reference program's by a relative error of at most 0.024.
Values may be sent and summed in bfloat16 or wider, within the bound.
No kernel may reach another device: no remote copies, remote signals or barrier semaphores. Data moves between devices by JAX's collectives and lax.ppermute only.
A program may use at most 128 MiB of HBM per device.

```python
import math
import jax
import jax.numpy as jnp
import numpy as np
from jax import lax

DR = 5120
HR = 40
HDR = 128
DF = 4096
HFW = 8
HDF = 256
CANDS = 8
LC = 8
LP = 32
PAIRS_DEV = 8
PD = 32
GROUPS = 32
PROMPTS = 1024
PAIRS = 256
FROWS = 24
N_TENSOR = 8


def draw_rank_query(key, part):
    own_key = jax.random.fold_in(key, 21)
    values_drawn = jnp.clip(jax.random.normal(own_key, (PAIRS, LP, HR, HDR)), -4.5, 4.5)
    return values_drawn.astype(jnp.float32).reshape(PAIRS, LP, HR * HDR).astype(jnp.bfloat16)


def draw_rank_key(key, part):
    own_key = jax.random.fold_in(key, 22)
    values_drawn = jnp.clip(jax.random.normal(own_key, (PAIRS, LP, HR, HDR)), -4.5, 4.5)
    return values_drawn.astype(jnp.float32).reshape(PAIRS, LP, HR * HDR).astype(jnp.bfloat16)


def draw_pair_index(key, part):
    prompt_key, first_key, step_key = jax.random.split(jax.random.fold_in(key, 31), 3)
    prompt = jax.random.randint(prompt_key, (PAIRS, 1), 0, PD)
    prompt = prompt.at[0, 0].set(PD - 1)
    first = jax.random.randint(first_key, (PAIRS, 1), 0, CANDS)
    stride = jax.random.randint(step_key, (PAIRS, 1), 1, CANDS)
    second = (first + stride) % CANDS
    return jnp.concatenate([prompt, first, second], axis=1).astype(jnp.int32)


def levels(key, dims, pieces, low, largest):
    def one(dim, blocks):
        heights = jax.random.uniform(jax.random.fold_in(jax.random.fold_in(key, 6), dim), (blocks,), jnp.float32, low / len(pieces), largest / len(pieces))
        return jnp.repeat(jnp.exp(heights), dims[dim] // blocks).reshape((-1,) + (1,) * (len(dims) - dim - 1))

    factor_of = one(*pieces[0])
    for cut in pieces[1:]:
        factor_of = factor_of * one(*cut)
    return factor_of


def length_profile(count, total, most, skew):
    portions = [(1 << 20) // math.isqrt(rank ** skew) + 1 for rank in range(2, count + 1)]
    rest, given = total - most - (count - 1), [1] * (count - 1)
    while rest > 0:
        candidates = [i for i in range(count - 1) if given[i] < most]
        whole, budget = sum([portions[i] for i in candidates]), rest
        for i in candidates:
            extra = min(most - given[i], max(1, budget * portions[i] // whole), rest)
            given[i] = given[i] + extra
            rest = rest - extra
    return np.array([most] + given)


def ragged_sizes(rng, count, total, reach, slope):
    if count == 2:
        one = jax.random.randint(rng, (), max(1, total - reach), min(reach, total - 1) + 1)
        return jnp.stack([one, total - one])
    tallies = jnp.asarray(length_profile(count, total, reach, slope), jnp.int32)
    couples = (count - 1) // 2
    source_of, taker = tallies[1:1 + 2 * couples:2], tallies[2:2 + 2 * couples:2]
    margin = jnp.minimum(source_of - 1, reach - taker)
    passed = jax.random.randint(jax.random.fold_in(rng, 1), (couples,), 0, 1 << 20) % (margin + 1)
    tallies = tallies.at[1:1 + 2 * couples:2].set(source_of - passed).at[2:2 + 2 * couples:2].set(taker + passed)
    return tallies[jax.random.permutation(jax.random.fold_in(rng, 2), count)]


def noise(key, shape, deviation, most, pieces=(), kind=jnp.bfloat16):
    array = deviation * jax.random.normal(key, shape, jnp.float32)
    if pieces:
        array = array * levels(key, shape, pieces, -0.22, 0.18)
    return jnp.clip(array, -most, most).astype(kind)


def setup_inputs(seed: int = 0) -> dict:
    splits = jax.random.split(jax.random.key(seed), 15)
    return {
        "rank_query": draw_rank_query(jax.random.fold_in(splits[14], 71), 0),
        "rank_key": draw_rank_key(jax.random.fold_in(splits[14], 71), 0),
        "rank_value": noise(splits[2], (PAIRS, LP, HR * HDR), 1.0, 6.0, ((0, 32), (2, 8))),
        "rank_resid": noise(splits[3], (PAIRS, LP, DR), 0.5, 4.0, ((0, 256),)),
        "out_weight": noise(splits[4], (HR * HDR, DR), (HR * HDR // 8) ** -0.5, 0.25, ((0, 8), (1, 32))),
        "rank_gain": jnp.clip(1.0 + 0.18 * jax.random.normal(splits[5], (DR,), jnp.float32), 0.099609375, 1.8984375).astype(jnp.bfloat16),
        "score_weight": noise(splits[6], (DR,), DR ** -0.5, 0.078125),
        "pair_index": draw_pair_index(jax.random.fold_in(splits[14], 71), 0),
        "cand_rank": jax.vmap(lambda own: jax.random.permutation(own, CANDS))(jax.random.split(splits[8], PROMPTS)).reshape((PROMPTS, CANDS)).astype(jnp.int32),
        "cand_len": jax.vmap(lambda own: ragged_sizes(own, CANDS, LC + (CANDS - 1) * (LC + 1) // 2, LC, 0))(jax.random.split(splits[9], PROMPTS)).reshape((PROMPTS, CANDS)).astype(jnp.int32),
        "blend_owner": jax.vmap(lambda own: jax.random.permutation(own, PD))(jax.random.split(splits[10], GROUPS)).reshape((GROUPS, PD)).astype(jnp.int32),
        "blend_rows": noise(splits[11], (PROMPTS, CANDS, LC, DF), 1.0, 6.0, ((0, 32), (3, 8))),
        "blend_gain": jnp.clip(1.0 + 0.18 * jax.random.normal(splits[12], (DF,), jnp.float32), 0.099609375, 1.8984375).astype(jnp.bfloat16),
        "blend_weight": noise(splits[13], (DF, 3, HFW * HDF), DF ** -0.5, 0.09375, ((0, 32), (2, 8))),
    }


def pair_attention(queries, keys_in, values_in):
    pair_count = queries.shape[0]
    query_heads = queries.astype(jnp.float32).reshape(pair_count, LP, HR, HDR)
    key_heads = keys_in.astype(jnp.float32).reshape(pair_count, LP, HR, HDR)
    value_heads = values_in.astype(jnp.float32).reshape(pair_count, LP, HR, HDR)
    scores = jnp.einsum('pihd,pjhd->phij', query_heads, key_heads, precision=lax.Precision.HIGHEST) * (1.0 / math.sqrt(HDR))
    highest = lax.optimization_barrier(jnp.max(scores, axis=-1, keepdims=True))
    weights = jnp.exp(scores - highest)
    soft_weights = (weights / lax.optimization_barrier(jnp.sum(weights, axis=-1, keepdims=True))).astype(jnp.bfloat16)
    context = jnp.einsum('phij,pjhd->pihd', soft_weights.astype(jnp.float32), value_heads, precision=lax.Precision.HIGHEST)
    return context.astype(jnp.bfloat16).reshape(pair_count * LP, HR * HDR)

def reference(rank_query, rank_key, rank_value, rank_resid, out_weight, rank_gain, score_weight, pair_index, cand_rank, cand_len, blend_owner, blend_rows, blend_gain, blend_weight):
    context = pair_attention(rank_query, rank_key, rank_value)
    group_width = HR * HDR // N_TENSOR
    mixed_rows = rank_resid.astype(jnp.float32).reshape(PAIRS * LP, DR)
    for group_index in range(N_TENSOR):
        head_part = jnp.dot(context[:, group_index * group_width:(group_index + 1) * group_width], out_weight[group_index * group_width:(group_index + 1) * group_width], preferred_element_type=jnp.float32)
        mixed_rows = mixed_rows + lax.optimization_barrier(head_part.astype(jnp.bfloat16)).astype(jnp.float32)
    mean_square = lax.optimization_barrier(jnp.mean(mixed_rows * mixed_rows, axis=-1, keepdims=True))
    normed = mixed_rows * lax.rsqrt(mean_square + 1e-05) * rank_gain.astype(jnp.float32)
    rank_hidden = normed.astype(jnp.bfloat16).reshape(PAIRS, LP, DR)
    leading = normed.reshape(PAIRS, LP, DR)[:, 0, :]
    pair_logit = lax.optimization_barrier(jnp.sum(leading * score_weight.astype(jnp.float32), axis=-1))
    pair_group = jnp.arange(PAIRS, dtype=jnp.int32) // PAIRS_DEV
    base_slot = pair_group * (PD * CANDS) + pair_index[:, 0] * CANDS
    slot_ids = jnp.arange(PROMPTS * CANDS, dtype=jnp.int32)
    upward = jnp.where((base_slot + pair_index[:, 1])[:, None] == slot_ids[None, :], pair_logit[:, None], 0.0)
    downward = jnp.where((base_slot + pair_index[:, 2])[:, None] == slot_ids[None, :], pair_logit[:, None], 0.0)
    cand_score = lax.optimization_barrier(jnp.sum(upward - downward, axis=0)).reshape(PROMPTS, CANDS)
    places = jnp.arange(3, dtype=jnp.int32)
    matched = cand_rank[:, None, :] == places[None, :, None]
    labels = jnp.arange(CANDS, dtype=jnp.int32)
    chosen = lax.optimization_barrier(jnp.sum(jnp.where(matched, labels[None, None, :], 0), axis=-1)).astype(jnp.int32)
    chosen_len = lax.optimization_barrier(jnp.sum(jnp.where(matched, cand_len[:, None, :], 0), axis=-1)).astype(jnp.int32)
    prompt_ids = jnp.arange(PROMPTS, dtype=jnp.int32)
    picked = blend_rows[prompt_ids[:, None], chosen]
    positions = jnp.arange(LC, dtype=jnp.int32)
    live_rows = positions[None, None, :] < chosen_len[:, :, None]
    picked = jnp.where(live_rows[..., None], picked, jnp.zeros((), jnp.bfloat16))
    flat_rows = picked.reshape(PROMPTS * FROWS, DF).astype(jnp.float32)
    scale_rows = lax.rsqrt(lax.optimization_barrier(jnp.mean(flat_rows * flat_rows, axis=-1, keepdims=True)) + 1e-06)
    blend_normed = (flat_rows * scale_rows * blend_gain.astype(jnp.float32)).astype(jnp.bfloat16)
    projected = jnp.dot(blend_normed, blend_weight.reshape(DF, 3 * HFW * HDF), preferred_element_type=jnp.float32)
    projected = projected.astype(jnp.bfloat16).reshape(PROMPTS, FROWS, 3, HFW * HDF)
    source_group = prompt_ids // PD
    destination = blend_owner.reshape(PROMPTS) * PD + source_group
    blended_qkv = jnp.zeros_like(projected).at[destination].set(projected)
    return (rank_hidden, cand_score, blended_qkv)
```

```python
import math

import jax
import jax.numpy as jnp
from jax import lax
from jax.experimental import pallas as pl
from jax.experimental.pallas import tpu as pltpu
from jax.sharding import Mesh, PartitionSpec as P

HR = 40
HDR = 128
NY, NX, NC, NZ = 4, 4, 2, 8
PLANE = ("y", "x", "core")


def ring(count, step):
    return [(i, (i + step) % count) for i in range(count)]


def pair_attention(queries, keys_in, values_in, head_count):
    pair_count, length, row_width = queries.shape
    head_size = row_width // head_count
    query_heads = queries.reshape(pair_count, length, head_count, head_size)
    key_heads = keys_in.reshape(pair_count, length, head_count, head_size)
    value_heads = values_in.reshape(pair_count, length, head_count, head_size)
    scores = jnp.einsum(
        "pihd,pjhd->phij", query_heads, key_heads, preferred_element_type=jnp.float32
    ) * (1.0 / math.sqrt(HDR))
    highest = jnp.max(scores, axis=-1, keepdims=True)
    weights = jnp.exp(scores - highest)
    soft_weights = (weights / jnp.sum(weights, axis=-1, keepdims=True)).astype(jnp.bfloat16)
    context = jnp.einsum(
        "phij,pjhd->pihd", soft_weights, value_heads, preferred_element_type=jnp.float32
    )
    return context.astype(jnp.bfloat16).reshape(pair_count * length, row_width)


def select_kernel(owner_ref, rank_ref, len_ref, rows_ref, out_ref):
    places = rank_ref.shape[0]
    position = lax.broadcasted_iota(jnp.int32, rows_ref.shape[1:], 0)

    def one_prompt(prompt, carry):
        owner = owner_ref[0, prompt]
        for rank in range(3):
            cand = jnp.int32(0)
            live = jnp.int32(0)
            for place in range(places):
                hit = rank_ref[place, prompt] == rank
                cand = jnp.where(hit, place, cand)
                live = jnp.where(hit, len_ref[place, prompt], live)
            picked = rows_ref[prompt * places + cand].astype(jnp.float32)
            out_ref[owner * 3 + rank] = jnp.where(position < live, picked, 0.0).astype(out_ref.dtype)
        return carry

    lax.fori_loop(0, owner_ref.shape[1], one_prompt, 0)


def select_rows(blend_owner, cand_rank, cand_len, blend_rows):
    prompts, cands, length, features = blend_rows.shape
    smem = pl.BlockSpec(memory_space=pltpu.SMEM)
    vmem = pl.BlockSpec(memory_space=pltpu.VMEM)
    return pl.pallas_call(
        select_kernel,
        out_shape=jax.ShapeDtypeStruct((prompts * 3, length, features), blend_rows.dtype),
        in_specs=[smem, smem, smem, vmem],
        out_specs=vmem,
        cost_estimate=pl.CostEstimate(flops=0, bytes_accessed=3 << 20, transcendentals=0),
    )(blend_owner, cand_rank.T, cand_len.T, blend_rows.reshape(prompts * cands, length, features))


def encode_kernel(where_ref, *refs):
    row_refs = refs[:NZ]
    mine_ref, other_ref, out_ref, weight_ref = refs[NZ:]
    third, depth, width = mine_ref.shape[1:]
    my_y, my_x, my_core, my_z = where_ref[0], where_ref[1], where_ref[2], where_ref[3]
    features = row_refs[0].shape[1]

    @pl.when(pl.program_id(0) == 0)
    def _():
        def one_source(order, carry):
            source = lax.rem(my_z + order, NZ)
            for piece in range(4):
                slab_y = source // 2
                slab_x = lax.rem(source, 2) * 2 + piece // 2
                slot = lax.rem(my_y - slab_y + NY, NY) * NX + lax.rem(my_x - slab_x + NX, NX)
                place = pl.ds(pl.multiple_of(order * features + piece * depth, depth), depth)

                @pl.when(my_core == piece % 2)
                def _():
                    for part in range(third):
                        weight_ref[part, place, :] = mine_ref[slot, part]

                @pl.when(my_core != piece % 2)
                def _():
                    for part in range(third):
                        weight_ref[part, place, :] = other_ref[slot, part]

            return carry

        lax.fori_loop(0, NZ, one_source, 0)

    squares = None
    for rows in row_refs:
        value = rows[...].astype(jnp.float32)
        term = jnp.sum(value * value, axis=-1, keepdims=True)
        squares = term if squares is None else squares + term
    scale = lax.rsqrt(squares * (1.0 / (NZ * features)) + 1e-06)
    prompts, length = out_ref.shape[0], out_ref.shape[2]
    for part in range(third):
        total = None
        for order, rows in enumerate(row_refs):
            term = jnp.dot(
                rows[...],
                weight_ref[part, order * features : (order + 1) * features, :],
                preferred_element_type=jnp.float32,
            )
            total = term if total is None else total + term
        total = (total * scale).astype(out_ref.dtype)
        out_ref[:, part] = total.reshape(prompts, length, width)


def encode(where, blocks, mine, other, prompts, length):
    rows, features = blocks[0].shape
    third, depth, width = mine.shape[1:]
    steps = 4
    step_rows = rows // steps
    step_prompts = prompts // steps
    row_spec = pl.BlockSpec((step_rows, features), lambda i, w: (i, 0))
    slab_spec = pl.BlockSpec(
        mine.shape, lambda i, w: (0, 0, 0, 0), pipeline_mode=pl.Buffered(1)
    )
    out = pl.pallas_call(
        encode_kernel,
        out_shape=jax.ShapeDtypeStruct((prompts, third, length, width), jnp.bfloat16),
        grid_spec=pltpu.PrefetchScalarGridSpec(
            num_scalar_prefetch=1,
            grid=(steps,),
            in_specs=[row_spec] * NZ + [slab_spec] * 2,
            out_specs=pl.BlockSpec(
                (step_prompts, third, length, width), lambda i, w: (i, 0, 0, 0)
            ),
            scratch_shapes=[pltpu.VMEM((third, NZ * features, width), jnp.bfloat16)],
        ),
        compiler_params=pltpu.CompilerParams(vmem_limit_bytes=40 << 20),
        cost_estimate=pl.CostEstimate(
            flops=2 * rows * NZ * features * third * width,
            bytes_accessed=16 << 20,
            transcendentals=rows,
        ),
    )(where, *blocks, mine, other)
    return out.transpose(0, 2, 1, 3)


def gather_axis(block, axis, count):
    before = lax.ppermute(block, axis, ring(count, 1))
    after = lax.ppermute(block, axis, ring(count, -1))
    across = lax.ppermute(before, axis, ring(count, 1))
    return jnp.concatenate([block, before, across, after], axis=0)


def body(
    rank_query,
    rank_key,
    rank_value,
    rank_resid,
    out_weight,
    rank_gain,
    score_weight,
    pair_index,
    cand_rank,
    cand_len,
    blend_owner,
    blend_rows,
    blend_gain,
    blend_weight,
):
    local_heads = HR // NZ
    length = rank_query.shape[1]
    my_y, my_x, my_core, my_z = (lax.axis_index(a) for a in ("y", "x", "core", "z"))

    outgoing = select_rows(blend_owner, cand_rank, cand_len, blend_rows)
    prompts = blend_rows.shape[0]
    features = blend_rows.shape[3]
    arrived = lax.all_to_all(
        outgoing.reshape(prompts, -1, features), PLANE, split_axis=0, concat_axis=0, tiled=True
    )
    picked_rows = arrived.shape[1]
    own = arrived.reshape(prompts * picked_rows, features)

    depth = blend_weight.shape[0]
    slab = (my_y * NX + my_x) * NC + my_core
    gain = lax.dynamic_slice_in_dim(blend_gain, slab * depth, depth, 0).astype(jnp.float32)
    own_slab = (blend_weight.transpose(1, 0, 2).astype(jnp.float32) * gain[None, :, None]).astype(
        jnp.bfloat16
    )
    mine = gather_axis(own_slab[None], "x", NX)
    mine = gather_axis(mine, "y", NY)
    other = lax.ppermute(mine, "core", ring(NC, 1))

    lower, upper = [own], [own]
    for step in range(3):
        lower.append(lax.ppermute(lower[-1], "z", ring(NZ, 1)))
        upper.append(lax.ppermute(upper[-1], "z", ring(NZ, -1)))
    half = own.shape[0] // 2
    across = jnp.concatenate(
        [
            lax.ppermute(lower[3][:half], "z", ring(NZ, 1)),
            lax.ppermute(upper[3][half:], "z", ring(NZ, -1)),
        ],
        axis=0,
    )
    blocks = [own, upper[1], upper[2], upper[3], across, lower[3], lower[2], lower[1]]
    where = jnp.stack([my_y, my_x, my_core, my_z]).astype(jnp.int32)
    blended_qkv = encode(where, blocks, mine, other, prompts, picked_rows)

    context = pair_attention(rank_query, rank_key, rank_value, local_heads)
    own_pairs = rank_resid.shape[0]
    own_rows = own_pairs * length
    term_rows = jnp.dot(
        context,
        lax.all_gather(out_weight, PLANE, axis=1, tiled=True),
        preferred_element_type=jnp.float32,
    )
    part_sum = lax.psum_scatter(
        term_rows.astype(jnp.bfloat16), "z", scatter_dimension=0, tiled=True
    ).astype(jnp.float32)
    mixed_rows = rank_resid.reshape(own_rows, -1).astype(jnp.float32) + part_sum
    mean_square = jnp.mean(mixed_rows * mixed_rows, axis=-1, keepdims=True)
    normed = mixed_rows * lax.rsqrt(mean_square + 1e-05) * rank_gain.astype(jnp.float32)
    rank_hidden = normed.astype(jnp.bfloat16).reshape(rank_resid.shape)
    leading = normed.reshape(own_pairs, length, -1)[:, 0, :]
    pair_logit = jnp.sum(leading * score_weight.astype(jnp.float32), axis=-1)
    prompt_count = cand_rank.shape[0]
    cand_count = cand_rank.shape[1]
    slot_ids = jnp.arange(prompt_count * cand_count, dtype=jnp.int32)
    base_slot = pair_index[:, 0] * cand_count
    upward = jnp.where(
        (base_slot + pair_index[:, 1])[:, None] == slot_ids[None, :], pair_logit[:, None], 0.0
    )
    downward = jnp.where(
        (base_slot + pair_index[:, 2])[:, None] == slot_ids[None, :], pair_logit[:, None], 0.0
    )
    cand_score = jnp.sum(upward - downward, axis=0).reshape(prompt_count, cand_count)
    for bit in (1, 2, 4):
        cand_score = cand_score + lax.ppermute(cand_score, "z", [(i, i ^ bit) for i in range(NZ)])
    return (rank_hidden, cand_score, blended_qkv)


def solution(mesh):
    grid = Mesh(mesh.devices.reshape(NY, NX, NC, NZ), ("y", "x", "core", "z"))
    whole = ("y", "x", "core", "z")
    placed = (
        P(PLANE, None, "z"),
        P(PLANE, None, "z"),
        P(PLANE, None, "z"),
        P(whole, None, None),
        P("z", PLANE),
        P(),
        P(),
        P(whole, None),
        P(PLANE, None),
        P(PLANE, None),
        P(PLANE, None),
        P(PLANE, None, None, "z"),
        P(),
        P(PLANE, None, "z"),
    )
    return jax.shard_map(
        body,
        mesh=grid,
        in_specs=placed,
        out_specs=(P(whole, None, None), P(PLANE, None), P(PLANE, None, None, "z")),
        check_vma=False,
    )
```

```python
import math

import jax
import jax.numpy as jnp
from jax import lax
from jax.experimental import pallas as pl
from jax.experimental.pallas import tpu as pltpu
from jax.sharding import Mesh, PartitionSpec as P

HR = 40
HDR = 128
NY, NX, NC, NZ = 4, 4, 2, 8
PLANE = ("y", "x", "core")


def ring(count, step):
    return [(i, (i + step) % count) for i in range(count)]


def pair_attention(queries, keys_in, values_in, head_count):
    pair_count, length, row_width = queries.shape
    head_size = row_width // head_count
    query_heads = queries.reshape(pair_count, length, head_count, head_size)
    key_heads = keys_in.reshape(pair_count, length, head_count, head_size)
    value_heads = values_in.reshape(pair_count, length, head_count, head_size)
    scores = jnp.einsum(
        "pihd,pjhd->phij", query_heads, key_heads, preferred_element_type=jnp.float32
    ) * (1.0 / math.sqrt(HDR))
    highest = jnp.max(scores, axis=-1, keepdims=True)
    weights = jnp.exp(scores - highest)
    soft_weights = (weights / jnp.sum(weights, axis=-1, keepdims=True)).astype(jnp.bfloat16)
    context = jnp.einsum(
        "phij,pjhd->pihd", soft_weights, value_heads, preferred_element_type=jnp.float32
    )
    return context.astype(jnp.bfloat16).reshape(pair_count * length, row_width)


def select_kernel(owner_ref, rank_ref, len_ref, rows_ref, out_ref):
    places = rank_ref.shape[0]
    position = lax.broadcasted_iota(jnp.int32, rows_ref.shape[1:], 0)

    def one_prompt(prompt, carry):
        owner = owner_ref[0, prompt]
        for rank in range(3):
            cand = jnp.int32(0)
            live = jnp.int32(0)
            for place in range(places):
                hit = rank_ref[place, prompt] == rank
                cand = jnp.where(hit, place, cand)
                live = jnp.where(hit, len_ref[place, prompt], live)
            picked = rows_ref[prompt * places + cand].astype(jnp.float32)
            out_ref[owner * 3 + rank] = jnp.where(position < live, picked, 0.0).astype(out_ref.dtype)
        return carry

    lax.fori_loop(0, owner_ref.shape[1], one_prompt, 0)


def select_rows(blend_owner, cand_rank, cand_len, blend_rows):
    prompts, cands, length, features = blend_rows.shape
    smem = pl.BlockSpec(memory_space=pltpu.SMEM)
    vmem = pl.BlockSpec(memory_space=pltpu.VMEM)
    return pl.pallas_call(
        select_kernel,
        out_shape=jax.ShapeDtypeStruct((prompts * 3, length, features), blend_rows.dtype),
        in_specs=[smem, smem, smem, vmem],
        out_specs=vmem,
        cost_estimate=pl.CostEstimate(flops=0, bytes_accessed=3 << 20, transcendentals=0),
    )(blend_owner, cand_rank.T, cand_len.T, blend_rows.reshape(prompts * cands, length, features))


def arrange_kernel(where_ref, *refs):
    slab_refs, out_ref = refs[:-1], refs[-1]
    third, depth = slab_refs[0].shape[1:3]
    my_y, my_x, my_core, my_z = where_ref[0], where_ref[1], where_ref[2], where_ref[3]
    for swapped in range(NC):
        for back in range(NY):
            slabs = slab_refs[swapped * NY + back]
            for left in range(NX):
                slab_y = lax.rem(my_y - back + NY, NY)
                slab_x = lax.rem(my_x - left + NX, NX)
                slab_core = lax.rem(my_core + swapped, NC)
                slab = (slab_y * NX + slab_x) * NC + slab_core
                order = lax.rem(slab // 4 - my_z + NZ, NZ)
                start = pl.multiple_of((order * 4 + lax.rem(slab, 4)) * depth, depth)
                for part in range(third):
                    out_ref[part, pl.ds(start, depth), :] = slabs[left, part]


def arrange(where, slabs):
    third, depth, width = slabs[0].shape[1:]
    vmem = pl.BlockSpec(memory_space=pltpu.VMEM)
    return pl.pallas_call(
        arrange_kernel,
        out_shape=jax.ShapeDtypeStruct((third, NC * NY * NX * depth, width), jnp.bfloat16),
        in_specs=[pl.BlockSpec(memory_space=pltpu.SMEM)] + [vmem] * len(slabs),
        out_specs=vmem,
        compiler_params=pltpu.CompilerParams(vmem_limit_bytes=32 << 20),
        cost_estimate=pl.CostEstimate(flops=0, bytes_accessed=12 << 20, transcendentals=0),
    )(where, *slabs)


def project_kernel(rows_ref, columns_ref, out_ref):
    out_ref[...] = lax.dot_general(
        rows_ref[...], columns_ref[...], (((1,), (1,)), ((), ())), preferred_element_type=jnp.float32
    ).astype(out_ref.dtype)


def project(rows, columns):
    count, depth = rows.shape
    width = columns.shape[0]
    steps = 4
    return pl.pallas_call(
        project_kernel,
        out_shape=jax.ShapeDtypeStruct((count, width), jnp.bfloat16),
        grid=(steps,),
        in_specs=[
            pl.BlockSpec((count, depth), lambda i: (0, 0)),
            pl.BlockSpec((width // steps, depth), lambda i: (i, 0)),
        ],
        out_specs=pl.BlockSpec((count, width // steps), lambda i: (0, i)),
        compiler_params=pltpu.CompilerParams(vmem_limit_bytes=16 << 20),
        cost_estimate=pl.CostEstimate(
            flops=2 * count * width * depth, bytes_accessed=9 << 20, transcendentals=0
        ),
    )(rows, columns)


def squares_of(values):
    value = values.astype(jnp.float32)
    return jnp.sum(value * value, axis=-1, keepdims=True)


def first_kernel(orders, *refs):
    row_refs = refs[: len(orders)]
    weight_ref, total_ref, squares_ref = refs[len(orders) :]
    features = row_refs[0].shape[1]
    squares = sum(squares_of(rows[...]) for rows in row_refs)
    squares_ref[...] = jnp.broadcast_to(squares, squares_ref.shape)
    for part in range(weight_ref.shape[0]):
        total_ref[part] = sum(
            jnp.dot(
                rows[...],
                weight_ref[part, order * features : (order + 1) * features, :],
                preferred_element_type=jnp.float32,
            )
            for order, rows in zip(orders, row_refs)
        )


def last_kernel(orders, row_a, row_b, low_ref, high_ref, weight_ref, total_ref, squares_ref, out_ref):
    features = row_a.shape[1]
    half_steps = pl.num_programs(0) // 2
    across = jnp.where(pl.program_id(0) < half_steps, low_ref[...], high_ref[...])
    values = [row_a[...], row_b[...], across]
    squares = squares_ref[:, :1] + sum(squares_of(value) for value in values)
    scale = lax.rsqrt(squares * (1.0 / (NZ * features)) + 1e-06)
    prompts, third, length, width = out_ref.shape
    for part in range(third):
        total = total_ref[part] + sum(
            jnp.dot(
                value,
                weight_ref[part, order * features : (order + 1) * features, :],
                preferred_element_type=jnp.float32,
            )
            for order, value in zip(orders, values)
        )
        out_ref[:, part] = (total * scale).astype(out_ref.dtype).reshape(prompts, length, width)


def whole_spec(array):
    return pl.BlockSpec(array.shape, lambda i: (0,) * array.ndim, pipeline_mode=pl.Buffered(1))


def encode_first(orders, blocks, weights):
    rows, features = blocks[0].shape
    third, _, width = weights.shape
    steps = 4
    step_rows = rows // steps
    return pl.pallas_call(
        lambda *refs: first_kernel(orders, *refs),
        out_shape=(
            jax.ShapeDtypeStruct((third, rows, width), jnp.float32),
            jax.ShapeDtypeStruct((rows, 128), jnp.float32),
        ),
        grid=(steps,),
        in_specs=[pl.BlockSpec((step_rows, features), lambda i: (i, 0))] * len(blocks)
        + [whole_spec(weights)],
        out_specs=(
            pl.BlockSpec((third, step_rows, width), lambda i: (0, i, 0)),
            pl.BlockSpec((step_rows, 128), lambda i: (i, 0)),
        ),
        compiler_params=pltpu.CompilerParams(vmem_limit_bytes=24 << 20),
        cost_estimate=pl.CostEstimate(
            flops=2 * rows * len(blocks) * features * third * width,
            bytes_accessed=12 << 20,
            transcendentals=0,
        ),
    )(*blocks, weights)


def encode_last(orders, row_a, row_b, low, high, weights, total, squares, prompts):
    rows, features = row_a.shape
    third, _, width = weights.shape
    length = rows // prompts
    steps = 4
    step_rows = rows // steps
    step_prompts = prompts // steps
    out = pl.pallas_call(
        lambda *refs: last_kernel(orders, *refs),
        out_shape=jax.ShapeDtypeStruct((prompts, third, length, width), jnp.bfloat16),
        grid=(steps,),
        in_specs=[
            pl.BlockSpec((step_rows, features), lambda i: (i, 0)),
            pl.BlockSpec((step_rows, features), lambda i: (i, 0)),
            pl.BlockSpec((step_rows, features), lambda i: (jnp.minimum(i, steps // 2 - 1), 0)),
            pl.BlockSpec((step_rows, features), lambda i: (jnp.maximum(i - steps // 2, 0), 0)),
            whole_spec(weights),
            pl.BlockSpec((third, step_rows, width), lambda i: (0, i, 0)),
            pl.BlockSpec((step_rows, 128), lambda i: (i, 0)),
        ],
        out_specs=pl.BlockSpec((step_prompts, third, length, width), lambda i: (i, 0, 0, 0)),
        compiler_params=pltpu.CompilerParams(vmem_limit_bytes=24 << 20),
        cost_estimate=pl.CostEstimate(
            flops=40 * rows * 3 * features * third * width,
            bytes_accessed=12 << 20,
            transcendentals=rows,
        ),
    )(row_a, row_b, low, high, weights, total, squares)
    return out.transpose(0, 2, 1, 3)


def norm_kernel(pair_ref, resid_ref, gain_ref, score_ref, sum_ref, hidden_ref, votes_ref):
    mixed = resid_ref[...].astype(jnp.float32) + sum_ref[...].astype(jnp.float32)
    squares = jnp.sum(mixed * mixed, axis=-1, keepdims=True)
    scale = lax.rsqrt(squares * (1.0 / mixed.shape[1]) + 1e-05)
    normed = mixed * scale * gain_ref[...].astype(jnp.float32)
    hidden_ref[...] = normed.astype(hidden_ref.dtype)
    logit = jnp.sum(normed[:1] * score_ref[...].astype(jnp.float32), axis=-1, keepdims=True)
    cand = lax.broadcasted_iota(jnp.int32, votes_ref.shape, 0)
    prompt = lax.broadcasted_iota(jnp.int32, votes_ref.shape, 1)
    own = prompt == pair_ref[0, 0]
    upward = jnp.where(own & (cand == pair_ref[0, 1]), logit, 0.0)
    downward = jnp.where(own & (cand == pair_ref[0, 2]), logit, 0.0)
    votes_ref[...] = upward - downward


def norm_and_vote(pair_index, resid, gain, score, part_sum, prompts, cands):
    rows, width = resid.shape
    vmem = pl.BlockSpec(memory_space=pltpu.VMEM)
    return pl.pallas_call(
        norm_kernel,
        out_shape=(
            jax.ShapeDtypeStruct((rows, width), jnp.bfloat16),
            jax.ShapeDtypeStruct((cands, prompts), jnp.float32),
        ),
        in_specs=[pl.BlockSpec(memory_space=pltpu.SMEM)] + [vmem] * 4,
        out_specs=(vmem, vmem),
        cost_estimate=pl.CostEstimate(
            flops=rows * width * 8, bytes_accessed=2 << 20, transcendentals=rows
        ),
    )(pair_index, resid, gain, score, part_sum)


def together(*values):
    return lax.optimization_barrier(values)


def body(
    rank_query,
    rank_key,
    rank_value,
    rank_resid,
    out_weight,
    rank_gain,
    score_weight,
    pair_index,
    cand_rank,
    cand_len,
    blend_owner,
    blend_rows,
    blend_gain,
    blend_weight,
):
    local_heads = HR // NZ
    length = rank_query.shape[1]
    my_y, my_x, my_core, my_z = (lax.axis_index(a) for a in ("y", "x", "core", "z"))

    where = jnp.stack([my_y, my_x, my_core, my_z]).astype(jnp.int32)
    columns = lax.all_gather(out_weight.T, PLANE, axis=0, tiled=True)

    outgoing = select_rows(blend_owner, cand_rank, cand_len, blend_rows)
    rank_query, blend_weight, outgoing = together(rank_query, blend_weight, outgoing)
    prompts = blend_rows.shape[0]
    features = blend_rows.shape[3]
    arrived = lax.all_to_all(
        outgoing.reshape(prompts, -1, features), PLANE, split_axis=0, concat_axis=0, tiled=True
    )
    own = arrived.reshape(prompts * arrived.shape[1], features)

    context = pair_attention(rank_query, rank_key, rank_value, local_heads)
    depth = blend_weight.shape[0]
    slab = (my_y * NX + my_x) * NC + my_core
    gain = lax.dynamic_slice_in_dim(blend_gain, slab * depth, depth, 0).astype(jnp.float32)
    own_slab = (blend_weight.transpose(1, 0, 2).astype(jnp.float32) * gain[None, :, None]).astype(
        jnp.bfloat16
    )[None]
    gain_row = rank_gain.reshape(1, -1)
    score_row = score_weight.reshape(1, -1)
    own, context, own_slab, gain_row, score_row, where = together(
        own, context, own_slab, gain_row, score_row, where
    )

    lower = lax.ppermute(own, "z", ring(NZ, 1))
    upper = lax.ppermute(own, "z", ring(NZ, -1))
    x_before = lax.ppermute(own_slab, "x", ring(NX, 1))
    x_after = lax.ppermute(own_slab, "x", ring(NX, -1))
    x_across = lax.ppermute(x_before, "x", ring(NX, 1))
    strip = jnp.concatenate([own_slab, x_before, x_across, x_after], axis=0)
    lower, upper, strip = together(lower, upper, strip)
    blocks = {1: upper, NZ - 1: lower, 0: own}

    lower = lax.ppermute(lower, "z", ring(NZ, 1))
    upper = lax.ppermute(upper, "z", ring(NZ, -1))
    y_before = lax.ppermute(strip, "y", ring(NY, 1))
    y_after = lax.ppermute(strip, "y", ring(NY, -1))
    term_rows = project(context, columns)
    lower, upper, y_before, y_after, term_rows = together(
        lower, upper, y_before, y_after, term_rows
    )
    blocks.update({2: upper, NZ - 2: lower})
    part_sum = lax.psum_scatter(term_rows, "z", scatter_dimension=0, tiled=True)

    lower = lax.ppermute(lower, "z", ring(NZ, 1))
    upper = lax.ppermute(upper, "z", ring(NZ, -1))
    y_across = jnp.concatenate(
        [
            lax.ppermute(y_before[:2], "y", ring(NY, 1)),
            lax.ppermute(y_after[2:], "y", ring(NY, -1)),
        ],
        axis=0,
    )
    lower, upper, y_across = together(lower, upper, y_across)

    slabs = [strip, y_before, y_across, y_after]
    weights = arrange(where, slabs + [lax.ppermute(s, "core", ring(NC, 1)) for s in slabs])
    near = (0, 1, 2, NZ - 2, NZ - 1)
    half = own.shape[0] // 2
    total, squares = encode_first(near, [blocks[i] for i in near], weights)
    low = lax.ppermute(lower[:half], "z", ring(NZ, 1))
    high = lax.ppermute(upper[half:], "z", ring(NZ, -1))
    blended_qkv = encode_last(
        (3, NZ - 3, 4), upper, lower, low, high, weights, total, squares, prompts
    )

    part_sum, blended_qkv = together(part_sum, blended_qkv)
    own_pairs = rank_resid.shape[0]
    rank_hidden, votes = norm_and_vote(
        pair_index,
        rank_resid.reshape(own_pairs * length, -1),
        gain_row,
        score_row,
        part_sum,
        prompts,
        cand_rank.shape[1],
    )
    rank_hidden = rank_hidden.reshape(rank_resid.shape)
    for bit in (1, 2, 4):
        votes = votes + lax.ppermute(votes, "z", [(i, i ^ bit) for i in range(NZ)])
    cand_score = votes.T
    return (rank_hidden, cand_score, blended_qkv)


def solution(mesh):
    grid = Mesh(mesh.devices.reshape(NY, NX, NC, NZ), ("y", "x", "core", "z"))
    whole = ("y", "x", "core", "z")
    placed = (
        P(PLANE, None, "z"),
        P(PLANE, None, "z"),
        P(PLANE, None, "z"),
        P(whole, None, None),
        P("z", PLANE),
        P(),
        P(),
        P(whole, None),
        P(PLANE, None),
        P(PLANE, None),
        P(PLANE, None),
        P(PLANE, None, None, "z"),
        P(),
        P(PLANE, None, "z"),
    )
    return jax.shard_map(
        body,
        mesh=grid,
        in_specs=placed,
        out_specs=(P(whole, None, None), P(PLANE, None), P(PLANE, None, None, "z")),
        check_vma=False,
    )
```

```python
import math

import jax
import jax.numpy as jnp
from jax import lax
from jax.experimental import pallas as pl
from jax.experimental.pallas import tpu as pltpu
from jax.sharding import Mesh, PartitionSpec as P

HR = 40
HDR = 128
NY, NX, NC, NZ = 4, 4, 2, 8
PLANE = ("y", "x", "core")


def ring(count, step):
    return [(i, (i + step) % count) for i in range(count)]


def pair_attention(queries, keys_in, values_in, head_count):
    pair_count, length, row_width = queries.shape
    head_size = row_width // head_count
    query_heads = queries.reshape(pair_count, length, head_count, head_size)
    key_heads = keys_in.reshape(pair_count, length, head_count, head_size)
    value_heads = values_in.reshape(pair_count, length, head_count, head_size)
    scores = jnp.einsum(
        "pihd,pjhd->phij", query_heads, key_heads, preferred_element_type=jnp.float32
    ) * (1.0 / math.sqrt(HDR))
    highest = jnp.max(scores, axis=-1, keepdims=True)
    weights = jnp.exp(scores - highest)
    soft_weights = (weights / jnp.sum(weights, axis=-1, keepdims=True)).astype(jnp.bfloat16)
    context = jnp.einsum(
        "phij,pjhd->pihd", soft_weights, value_heads, preferred_element_type=jnp.float32
    )
    return context.astype(jnp.bfloat16).reshape(pair_count * length, row_width)


def select_kernel(owner_ref, rank_ref, len_ref, rows_ref, out_ref):
    places = rank_ref.shape[0]
    position = lax.broadcasted_iota(jnp.int32, rows_ref.shape[1:], 0)

    def one_prompt(prompt, carry):
        owner = owner_ref[0, prompt]
        for rank in range(3):
            cand = jnp.int32(0)
            live = jnp.int32(0)
            for place in range(places):
                hit = rank_ref[place, prompt] == rank
                cand = jnp.where(hit, place, cand)
                live = jnp.where(hit, len_ref[place, prompt], live)
            picked = rows_ref[prompt * places + cand].astype(jnp.float32)
            out_ref[owner * 3 + rank] = jnp.where(position < live, picked, 0.0).astype(out_ref.dtype)
        return carry

    lax.fori_loop(0, owner_ref.shape[1], one_prompt, 0)


def select_rows(blend_owner, cand_rank, cand_len, blend_rows):
    prompts, cands, length, features = blend_rows.shape
    smem = pl.BlockSpec(memory_space=pltpu.SMEM)
    vmem = pl.BlockSpec(memory_space=pltpu.VMEM)
    return pl.pallas_call(
        select_kernel,
        out_shape=jax.ShapeDtypeStruct((prompts * 3, length, features), blend_rows.dtype),
        in_specs=[smem, smem, smem, vmem],
        out_specs=vmem,
        cost_estimate=pl.CostEstimate(flops=0, bytes_accessed=3 << 20, transcendentals=0),
    )(blend_owner, cand_rank.T, cand_len.T, blend_rows.reshape(prompts * cands, length, features))


def arrange_kernel(where_ref, *refs):
    slab_refs, out_ref = refs[:-1], refs[-1]
    third, depth = slab_refs[0].shape[1:3]
    my_y, my_x, my_core, my_z = where_ref[0], where_ref[1], where_ref[2], where_ref[3]
    for swapped in range(NC):
        for back in range(NY):
            slabs = slab_refs[swapped * NY + back]
            for left in range(NX):
                slab_y = lax.rem(my_y - back + NY, NY)
                slab_x = lax.rem(my_x - left + NX, NX)
                slab_core = lax.rem(my_core + swapped, NC)
                slab = (slab_y * NX + slab_x) * NC + slab_core
                order = lax.rem(slab // 4 - my_z + NZ, NZ)
                start = pl.multiple_of((order * 4 + lax.rem(slab, 4)) * depth, depth)
                for part in range(third):
                    out_ref[part, pl.ds(start, depth), :] = slabs[left, part]


def arrange(where, slabs):
    third, depth, width = slabs[0].shape[1:]
    vmem = pl.BlockSpec(memory_space=pltpu.VMEM)
    return pl.pallas_call(
        arrange_kernel,
        out_shape=jax.ShapeDtypeStruct((third, NC * NY * NX * depth, width), jnp.bfloat16),
        in_specs=[pl.BlockSpec(memory_space=pltpu.SMEM)] + [vmem] * len(slabs),
        out_specs=vmem,
        compiler_params=pltpu.CompilerParams(vmem_limit_bytes=32 << 20),
        cost_estimate=pl.CostEstimate(flops=0, bytes_accessed=12 << 20, transcendentals=0),
    )(where, *slabs)


def project_kernel(rows_ref, columns_ref, out_ref, lead_ref):
    product = lax.dot_general(
        rows_ref[...], columns_ref[...], (((1,), (1,)), ((), ())), preferred_element_type=jnp.float32
    )
    out_ref[...] = product.astype(out_ref.dtype)
    pairs = lead_ref.shape[0]
    length = product.shape[0] // pairs
    for pair in range(pairs):
        row = product[pair * length : pair * length + 1].astype(out_ref.dtype)
        lead_ref[pair : pair + 1] = row.astype(lead_ref.dtype)


def project(rows, columns, pairs):
    count, depth = rows.shape
    width = columns.shape[0]
    steps = 4
    return pl.pallas_call(
        project_kernel,
        out_shape=(
            jax.ShapeDtypeStruct((count, width), jnp.bfloat16),
            jax.ShapeDtypeStruct((pairs, width), jnp.float32),
        ),
        grid=(steps,),
        in_specs=[
            pl.BlockSpec((count, depth), lambda i: (0, 0)),
            pl.BlockSpec((width // steps, depth), lambda i: (i, 0)),
        ],
        out_specs=(
            pl.BlockSpec((count, width // steps), lambda i: (0, i)),
            pl.BlockSpec((pairs, width // steps), lambda i: (0, i)),
        ),
        compiler_params=pltpu.CompilerParams(vmem_limit_bytes=16 << 20),
        cost_estimate=pl.CostEstimate(
            flops=2 * count * width * depth, bytes_accessed=9 << 20, transcendentals=0
        ),
    )(rows, columns)


def squares_of(values):
    value = values.astype(jnp.float32)
    return jnp.sum(value * value, axis=-1, keepdims=True)


def first_kernel(orders, *refs):
    row_refs = refs[: len(orders)]
    weight_ref, total_ref, squares_ref = refs[len(orders) :]
    features = row_refs[0].shape[1]
    squares = sum(squares_of(rows[...]) for rows in row_refs)
    squares_ref[...] = jnp.broadcast_to(squares, squares_ref.shape)
    for part in range(weight_ref.shape[0]):
        total_ref[part] = sum(
            jnp.dot(
                rows[...],
                weight_ref[part, order * features : (order + 1) * features, :],
                preferred_element_type=jnp.float32,
            )
            for order, rows in zip(orders, row_refs)
        )


def last_kernel(orders, row_a, row_b, low_ref, high_ref, weight_ref, total_ref, squares_ref, out_ref):
    features = row_a.shape[1]
    half_steps = pl.num_programs(0) // 2
    across = jnp.where(pl.program_id(0) < half_steps, low_ref[...], high_ref[...])
    values = [row_a[...], row_b[...], across]
    squares = squares_ref[:, :1] + sum(squares_of(value) for value in values)
    scale = lax.rsqrt(squares * (1.0 / (NZ * features)) + 1e-06)
    prompts, third, length, width = out_ref.shape
    for part in range(third):
        total = total_ref[part] + sum(
            jnp.dot(
                value,
                weight_ref[part, order * features : (order + 1) * features, :],
                preferred_element_type=jnp.float32,
            )
            for order, value in zip(orders, values)
        )
        out_ref[:, part] = (total * scale).astype(out_ref.dtype).reshape(prompts, length, width)


def whole_spec(array):
    return pl.BlockSpec(array.shape, lambda i: (0,) * array.ndim, pipeline_mode=pl.Buffered(1))


def encode_first(orders, blocks, weights):
    rows, features = blocks[0].shape
    third, _, width = weights.shape
    steps = 4
    step_rows = rows // steps
    return pl.pallas_call(
        lambda *refs: first_kernel(orders, *refs),
        out_shape=(
            jax.ShapeDtypeStruct((third, rows, width), jnp.float32),
            jax.ShapeDtypeStruct((rows, 128), jnp.float32),
        ),
        grid=(steps,),
        in_specs=[pl.BlockSpec((step_rows, features), lambda i: (i, 0))] * len(blocks)
        + [whole_spec(weights)],
        out_specs=(
            pl.BlockSpec((third, step_rows, width), lambda i: (0, i, 0)),
            pl.BlockSpec((step_rows, 128), lambda i: (i, 0)),
        ),
        compiler_params=pltpu.CompilerParams(vmem_limit_bytes=24 << 20),
        cost_estimate=pl.CostEstimate(
            flops=2 * rows * len(blocks) * features * third * width,
            bytes_accessed=12 << 20,
            transcendentals=0,
        ),
    )(*blocks, weights)


def encode_last(orders, row_a, row_b, low, high, weights, total, squares, prompts):
    rows, features = row_a.shape
    third, _, width = weights.shape
    length = rows // prompts
    steps = 4
    step_rows = rows // steps
    step_prompts = prompts // steps
    out = pl.pallas_call(
        lambda *refs: last_kernel(orders, *refs),
        out_shape=jax.ShapeDtypeStruct((prompts, third, length, width), jnp.bfloat16),
        grid=(steps,),
        in_specs=[
            pl.BlockSpec((step_rows, features), lambda i: (i, 0)),
            pl.BlockSpec((step_rows, features), lambda i: (i, 0)),
            pl.BlockSpec((step_rows, features), lambda i: (jnp.minimum(i, steps // 2 - 1), 0)),
            pl.BlockSpec((step_rows, features), lambda i: (jnp.maximum(i - steps // 2, 0), 0)),
            whole_spec(weights),
            pl.BlockSpec((third, step_rows, width), lambda i: (0, i, 0)),
            pl.BlockSpec((step_rows, 128), lambda i: (i, 0)),
        ],
        out_specs=pl.BlockSpec((step_prompts, third, length, width), lambda i: (i, 0, 0, 0)),
        compiler_params=pltpu.CompilerParams(vmem_limit_bytes=24 << 20),
        cost_estimate=pl.CostEstimate(
            flops=40 * rows * 3 * features * third * width,
            bytes_accessed=12 << 20,
            transcendentals=rows,
        ),
    )(row_a, row_b, low, high, weights, total, squares)
    return out.transpose(0, 2, 1, 3)


def norm_kernel(resid_ref, gain_ref, sum_ref, hidden_ref):
    mixed = resid_ref[...].astype(jnp.float32) + sum_ref[...].astype(jnp.float32)
    squares = jnp.sum(mixed * mixed, axis=-1, keepdims=True)
    scale = lax.rsqrt(squares * (1.0 / mixed.shape[1]) + 1e-05)
    normed = mixed * scale * gain_ref[...].astype(jnp.float32)
    hidden_ref[...] = normed.astype(hidden_ref.dtype)


def norm(resid, gain, part_sum):
    rows, width = resid.shape
    vmem = pl.BlockSpec(memory_space=pltpu.VMEM)
    return pl.pallas_call(
        norm_kernel,
        out_shape=jax.ShapeDtypeStruct((rows, width), jnp.bfloat16),
        in_specs=[vmem] * 3,
        out_specs=vmem,
        cost_estimate=pl.CostEstimate(
            flops=rows * width * 8, bytes_accessed=2 << 20, transcendentals=rows
        ),
    )(resid, gain, part_sum)


def vote_kernel(gain_ref, score_ref, lead_ref, votes_ref):
    pairs, width = lead_ref.shape[0], gain_ref.shape[1]
    mixed = lead_ref[:, :width].astype(jnp.float32)
    squares = jnp.sum(mixed * mixed, axis=-1, keepdims=True)
    scale = lax.rsqrt(squares * (1.0 / width) + 1e-05)
    normed = mixed * scale * gain_ref[...].astype(jnp.float32)
    logits = jnp.sum(normed * score_ref[...].astype(jnp.float32), axis=-1, keepdims=True)
    index = lead_ref[:, width:].astype(jnp.float32)
    cand = lax.broadcasted_iota(jnp.int32, votes_ref.shape, 0).astype(jnp.float32)
    prompt = lax.broadcasted_iota(jnp.int32, votes_ref.shape, 1).astype(jnp.float32)
    votes = jnp.zeros(votes_ref.shape, jnp.float32)
    for pair in range(pairs):
        own = prompt == index[pair : pair + 1, 0:1]
        logit = logits[pair : pair + 1]
        votes = votes + jnp.where(own & (cand == index[pair : pair + 1, 1:2]), logit, 0.0)
        votes = votes - jnp.where(own & (cand == index[pair : pair + 1, 2:3]), logit, 0.0)
    votes_ref[...] = votes


def vote(gain, score, lead, prompts, cands):
    vmem = pl.BlockSpec(memory_space=pltpu.VMEM)
    return pl.pallas_call(
        vote_kernel,
        out_shape=jax.ShapeDtypeStruct((cands, prompts), jnp.float32),
        in_specs=[vmem] * 3,
        out_specs=vmem,
    )(gain, score, lead)


def exchange(partial, bit):
    sent = lax.ppermute(partial.astype(jnp.bfloat16), "z", [(i, i ^ bit) for i in range(NZ)])
    return partial + sent.astype(jnp.float32)


def together(*values):
    return lax.optimization_barrier(values)


def body(
    rank_query,
    rank_key,
    rank_value,
    rank_resid,
    out_weight,
    rank_gain,
    score_weight,
    pair_index,
    cand_rank,
    cand_len,
    blend_owner,
    blend_rows,
    blend_gain,
    blend_weight,
):
    local_heads = HR // NZ
    length = rank_query.shape[1]
    my_y, my_x, my_core, my_z = (lax.axis_index(a) for a in ("y", "x", "core", "z"))

    where = jnp.stack([my_y, my_x, my_core, my_z]).astype(jnp.int32)
    columns = lax.all_gather(out_weight.T, PLANE, axis=0, tiled=True)

    outgoing = select_rows(blend_owner, cand_rank, cand_len, blend_rows)
    rank_query, blend_weight, outgoing = together(rank_query, blend_weight, outgoing)
    prompts = blend_rows.shape[0]
    features = blend_rows.shape[3]
    arrived = lax.all_to_all(
        outgoing.reshape(prompts, -1, features), PLANE, split_axis=0, concat_axis=0, tiled=True
    )
    own = arrived.reshape(prompts * arrived.shape[1], features)

    context = pair_attention(rank_query, rank_key, rank_value, local_heads)
    depth = blend_weight.shape[0]
    slab = (my_y * NX + my_x) * NC + my_core
    gain = lax.dynamic_slice_in_dim(blend_gain, slab * depth, depth, 0).astype(jnp.float32)
    own_slab = (blend_weight.transpose(1, 0, 2).astype(jnp.float32) * gain[None, :, None]).astype(
        jnp.bfloat16
    )[None]
    gain_row = rank_gain.reshape(1, -1)
    score_row = score_weight.reshape(1, -1)
    own, context, own_slab, gain_row, score_row, where = together(
        own, context, own_slab, gain_row, score_row, where
    )

    lower = lax.ppermute(own, "z", ring(NZ, 1))
    upper = lax.ppermute(own, "z", ring(NZ, -1))
    x_before = lax.ppermute(own_slab, "x", ring(NX, 1))
    x_after = lax.ppermute(own_slab, "x", ring(NX, -1))
    x_across = lax.ppermute(x_before, "x", ring(NX, 1))
    strip = jnp.concatenate([own_slab, x_before, x_across, x_after], axis=0)
    lower, upper, strip = together(lower, upper, strip)
    blocks = {1: upper, NZ - 1: lower, 0: own}

    lower = lax.ppermute(lower, "z", ring(NZ, 1))
    upper = lax.ppermute(upper, "z", ring(NZ, -1))
    y_before = lax.ppermute(strip, "y", ring(NY, 1))
    y_after = lax.ppermute(strip, "y", ring(NY, -1))
    term_rows, lead = project(context, columns, NZ)
    lower, upper, y_before, y_after, lead = together(lower, upper, y_before, y_after, lead)
    blocks.update({2: upper, NZ - 2: lower})
    part_sum = lax.psum_scatter(term_rows, "z", scatter_dimension=0, tiled=True)

    lower = lax.ppermute(lower, "z", ring(NZ, 1))
    upper = lax.ppermute(upper, "z", ring(NZ, -1))
    y_across = jnp.concatenate(
        [
            lax.ppermute(y_before[:2], "y", ring(NY, 1)),
            lax.ppermute(y_after[2:], "y", ring(NY, -1)),
        ],
        axis=0,
    )
    pair = lax.broadcasted_iota(jnp.int32, (NZ, 1), 0)
    own_lead = jnp.concatenate(
        [rank_resid[:, 0].astype(jnp.float32), jnp.pad(pair_index, ((0, 0), (0, 125))).astype(jnp.float32)],
        axis=1,
    )
    lead = jnp.pad(lead, ((0, 0), (0, 128))) + jnp.where(pair == my_z, own_lead, 0.0)
    lead = exchange(lead, 1)
    lower, upper, y_across, lead = together(lower, upper, y_across, lead)

    slabs = [strip, y_before, y_across, y_after]
    weights = arrange(where, slabs + [lax.ppermute(s, "core", ring(NC, 1)) for s in slabs])
    near = (0, 1, 2, NZ - 2, NZ - 1)
    half = own.shape[0] // 2
    total, squares = encode_first(near, [blocks[i] for i in near], weights)
    low = lax.ppermute(lower[:half], "z", ring(NZ, 1))
    high = lax.ppermute(upper[half:], "z", ring(NZ, -1))
    lead = exchange(lead, 2)
    low, high, lead, part_sum = together(low, high, lead, part_sum)
    blended_qkv = encode_last(
        (3, NZ - 3, 4), upper, lower, low, high, weights, total, squares, prompts
    )

    lead = exchange(lead, 4)
    votes = vote(gain_row, score_row, lead, prompts, cand_rank.shape[1])

    cand_score = votes.T
    own_pairs = rank_resid.shape[0]
    rank_hidden = norm(rank_resid.reshape(own_pairs * length, -1), gain_row, part_sum)
    rank_hidden = rank_hidden.reshape(rank_resid.shape)
    return (rank_hidden, cand_score, blended_qkv)


def solution(mesh):
    grid = Mesh(mesh.devices.reshape(NY, NX, NC, NZ), ("y", "x", "core", "z"))
    whole = ("y", "x", "core", "z")
    placed = (
        P(PLANE, None, "z"),
        P(PLANE, None, "z"),
        P(PLANE, None, "z"),
        P(whole, None, None),
        P("z", PLANE),
        P(),
        P(),
        P(whole, None),
        P(PLANE, None),
        P(PLANE, None),
        P(PLANE, None),
        P(PLANE, None, None, "z"),
        P(),
        P(PLANE, None, "z"),
    )
    return jax.shard_map(
        body,
        mesh=grid,
        in_specs=placed,
        out_specs=(P(whole, None, None), P(PLANE, None), P(PLANE, None, None, "z")),
        check_vma=False,
    )
```

```python
import math

import jax
import jax.numpy as jnp
from jax import lax
from jax.experimental import pallas as pl
from jax.experimental.pallas import tpu as pltpu
from jax.sharding import Mesh, PartitionSpec as P

HR = 40
HDR = 128
NY, NX, NC, NZ = 4, 4, 2, 8
PLANE = ("y", "x", "core")


def ring(count, step):
    return [(i, (i + step) % count) for i in range(count)]


def pair_attention(queries, keys_in, values_in, head_count):
    pair_count, length, row_width = queries.shape
    head_size = row_width // head_count
    query_heads = queries.reshape(pair_count, length, head_count, head_size)
    key_heads = keys_in.reshape(pair_count, length, head_count, head_size)
    value_heads = values_in.reshape(pair_count, length, head_count, head_size)
    scores = jnp.einsum(
        "pihd,pjhd->phij", query_heads, key_heads, preferred_element_type=jnp.float32
    ) * (1.0 / math.sqrt(HDR))
    highest = jnp.max(scores, axis=-1, keepdims=True)
    weights = jnp.exp(scores - highest)
    soft_weights = (weights / jnp.sum(weights, axis=-1, keepdims=True)).astype(jnp.bfloat16)
    context = jnp.einsum(
        "phij,pjhd->pihd", soft_weights, value_heads, preferred_element_type=jnp.float32
    )
    return context.astype(jnp.bfloat16).reshape(pair_count * length, row_width)


def select_kernel(owner_ref, rank_ref, len_ref, rows_ref, out_ref, cand_ref, live_ref):
    places = rank_ref.shape[0]
    position = lax.broadcasted_iota(jnp.int32, rows_ref.shape[1:], 0)

    def one_prompt(prompt, carry):
        owner = owner_ref[0, prompt]
        for place in range(places):
            rank = rank_ref[place, prompt]
            cand_ref[prompt, rank] = place
            live_ref[prompt, rank] = len_ref[place, prompt]
        for rank in range(3):
            picked = rows_ref[prompt * places + cand_ref[prompt, rank]].astype(jnp.float32)
            chosen = jnp.where(position < live_ref[prompt, rank], picked, 0.0)
            out_ref[owner * 3 + rank] = chosen.astype(out_ref.dtype)
        return carry

    lax.fori_loop(0, owner_ref.shape[1], one_prompt, 0, unroll=4)


def select_rows(blend_owner, cand_rank, cand_len, blend_rows):
    prompts, cands, length, features = blend_rows.shape
    smem = pl.BlockSpec(memory_space=pltpu.SMEM)
    vmem = pl.BlockSpec(memory_space=pltpu.VMEM)
    return pl.pallas_call(
        select_kernel,
        out_shape=jax.ShapeDtypeStruct((prompts * 3, length, features), blend_rows.dtype),
        in_specs=[smem, smem, smem, vmem],
        out_specs=vmem,
        scratch_shapes=[pltpu.SMEM((prompts, cands), jnp.int32)] * 2,
        cost_estimate=pl.CostEstimate(flops=0, bytes_accessed=3 << 20, transcendentals=0),
    )(blend_owner, cand_rank.T, cand_len.T, blend_rows.reshape(prompts * cands, length, features))


def arrange_kernel(where_ref, token_ref, *refs):
    slab_refs, out_ref = refs[:-1], refs[-1]
    third, depth = slab_refs[0].shape[1:3]
    my_y, my_x, my_core, my_z = where_ref[0], where_ref[1], where_ref[2], where_ref[3]
    for swapped in range(NC):
        for back in range(NY):
            slabs = slab_refs[swapped * NY + back]
            for left in range(NX):
                slab_y = lax.rem(my_y - back + NY, NY)
                slab_x = lax.rem(my_x - left + NX, NX)
                slab_core = lax.rem(my_core + swapped, NC)
                slab = (slab_y * NX + slab_x) * NC + slab_core
                order = lax.rem(slab // 4 - my_z + NZ, NZ)
                start = pl.multiple_of((order * 4 + lax.rem(slab, 4)) * depth, depth)
                for part in range(third):
                    out_ref[part, pl.ds(start, depth), :] = slabs[left, part]


def arrange(where, token, slabs):
    third, depth, width = slabs[0].shape[1:]
    vmem = pl.BlockSpec(memory_space=pltpu.VMEM)
    return pl.pallas_call(
        arrange_kernel,
        out_shape=jax.ShapeDtypeStruct((third, NC * NY * NX * depth, width), jnp.bfloat16),
        in_specs=[pl.BlockSpec(memory_space=pltpu.SMEM)] + [vmem] * (len(slabs) + 1),
        out_specs=vmem,
        compiler_params=pltpu.CompilerParams(vmem_limit_bytes=32 << 20),
        cost_estimate=pl.CostEstimate(flops=0, bytes_accessed=12 << 20, transcendentals=0),
    )(where, token, *slabs)


def project_kernel(rows_ref, columns_ref, out_ref, token_ref):
    token_ref[...] = jnp.zeros_like(token_ref)
    out_ref[...] = lax.dot_general(
        rows_ref[...], columns_ref[...], (((1,), (1,)), ((), ())), preferred_element_type=jnp.float32
    ).astype(out_ref.dtype)


def project(rows, columns):
    count, depth = rows.shape
    width = columns.shape[0]
    steps = 4
    return pl.pallas_call(
        project_kernel,
        out_shape=(
            jax.ShapeDtypeStruct((count, width), jnp.bfloat16),
            jax.ShapeDtypeStruct((8, 128), jnp.float32),
        ),
        grid=(steps,),
        in_specs=[
            pl.BlockSpec((count, depth), lambda i: (0, 0)),
            pl.BlockSpec((width // steps, depth), lambda i: (i, 0)),
        ],
        out_specs=(
            pl.BlockSpec((count, width // steps), lambda i: (0, i)),
            pl.BlockSpec((8, 128), lambda i: (0, 0)),
        ),
        compiler_params=pltpu.CompilerParams(vmem_limit_bytes=16 << 20),
        cost_estimate=pl.CostEstimate(
            flops=2 * count * width * depth, bytes_accessed=9 << 20, transcendentals=0
        ),
    )(rows, columns)


def squares_of(values):
    value = values.astype(jnp.float32)
    return jnp.sum(value * value, axis=-1, keepdims=True)


def first_kernel(orders, *refs):
    row_refs = refs[: len(orders)]
    weight_ref, total_ref, squares_ref = refs[len(orders) :]
    features = row_refs[0].shape[1]
    squares = sum(squares_of(rows[...]) for rows in row_refs)
    squares_ref[...] = jnp.broadcast_to(squares, squares_ref.shape)
    for part in range(weight_ref.shape[0]):
        total_ref[part] = sum(
            jnp.dot(
                rows[...],
                weight_ref[part, order * features : (order + 1) * features, :],
                preferred_element_type=jnp.float32,
            )
            for order, rows in zip(orders, row_refs)
        )


def last_kernel(orders, row_a, row_b, low_ref, high_ref, weight_ref, total_ref, squares_ref, out_ref):
    features = row_a.shape[1]
    half_steps = pl.num_programs(0) // 2
    across = jnp.where(pl.program_id(0) < half_steps, low_ref[...], high_ref[...])
    values = [row_a[...], row_b[...], across]
    squares = squares_ref[:, :1] + sum(squares_of(value) for value in values)
    scale = lax.rsqrt(squares * (1.0 / (NZ * features)) + 1e-06)
    prompts, third, length, width = out_ref.shape
    for part in range(third):
        total = total_ref[part] + sum(
            jnp.dot(
                value,
                weight_ref[part, order * features : (order + 1) * features, :],
                preferred_element_type=jnp.float32,
            )
            for order, value in zip(orders, values)
        )
        out_ref[:, part] = (total * scale).astype(out_ref.dtype).reshape(prompts, length, width)


def whole_spec(array):
    return pl.BlockSpec(array.shape, lambda i: (0,) * array.ndim, pipeline_mode=pl.Buffered(1))


def encode_first(orders, blocks, weights):
    rows, features = blocks[0].shape
    third, _, width = weights.shape
    steps = 4
    step_rows = rows // steps
    return pl.pallas_call(
        lambda *refs: first_kernel(orders, *refs),
        out_shape=(
            jax.ShapeDtypeStruct((third, rows, width), jnp.float32),
            jax.ShapeDtypeStruct((rows, 128), jnp.float32),
        ),
        grid=(steps,),
        in_specs=[pl.BlockSpec((step_rows, features), lambda i: (i, 0))] * len(blocks)
        + [whole_spec(weights)],
        out_specs=(
            pl.BlockSpec((third, step_rows, width), lambda i: (0, i, 0)),
            pl.BlockSpec((step_rows, 128), lambda i: (i, 0)),
        ),
        compiler_params=pltpu.CompilerParams(vmem_limit_bytes=24 << 20),
        cost_estimate=pl.CostEstimate(
            flops=2 * rows * len(blocks) * features * third * width,
            bytes_accessed=12 << 20,
            transcendentals=0,
        ),
    )(*blocks, weights)


def encode_last(orders, row_a, row_b, low, high, weights, total, squares, prompts):
    rows, features = row_a.shape
    third, _, width = weights.shape
    length = rows // prompts
    steps = 4
    step_rows = rows // steps
    step_prompts = prompts // steps
    out = pl.pallas_call(
        lambda *refs: last_kernel(orders, *refs),
        out_shape=jax.ShapeDtypeStruct((prompts, third, length, width), jnp.bfloat16),
        grid=(steps,),
        in_specs=[
            pl.BlockSpec((step_rows, features), lambda i: (i, 0)),
            pl.BlockSpec((step_rows, features), lambda i: (i, 0)),
            pl.BlockSpec((step_rows, features), lambda i: (jnp.minimum(i, steps // 2 - 1), 0)),
            pl.BlockSpec((step_rows, features), lambda i: (jnp.maximum(i - steps // 2, 0), 0)),
            whole_spec(weights),
            pl.BlockSpec((third, step_rows, width), lambda i: (0, i, 0)),
            pl.BlockSpec((step_rows, 128), lambda i: (i, 0)),
        ],
        out_specs=pl.BlockSpec((step_prompts, third, length, width), lambda i: (i, 0, 0, 0)),
        compiler_params=pltpu.CompilerParams(vmem_limit_bytes=24 << 20),
        cost_estimate=pl.CostEstimate(
            flops=40 * rows * 3 * features * third * width,
            bytes_accessed=12 << 20,
            transcendentals=rows,
        ),
    )(row_a, row_b, low, high, weights, total, squares)
    return out.transpose(0, 2, 1, 3)


def norm_kernel(pair_ref, resid_ref, gain_ref, score_ref, sum_ref, hidden_ref, votes_ref):
    mixed = resid_ref[...].astype(jnp.float32) + sum_ref[...].astype(jnp.float32)
    squares = jnp.sum(mixed * mixed, axis=-1, keepdims=True)
    scale = lax.rsqrt(squares * (1.0 / mixed.shape[1]) + 1e-05)
    normed = mixed * scale * gain_ref[...].astype(jnp.float32)
    hidden_ref[...] = normed.astype(hidden_ref.dtype)
    logit = jnp.sum(normed[:1] * score_ref[...].astype(jnp.float32), axis=-1, keepdims=True)
    cand = lax.broadcasted_iota(jnp.int32, votes_ref.shape, 0)
    prompt = lax.broadcasted_iota(jnp.int32, votes_ref.shape, 1)
    own = prompt == pair_ref[0, 0]
    upward = jnp.where(own & (cand == pair_ref[0, 1]), logit, 0.0)
    downward = jnp.where(own & (cand == pair_ref[0, 2]), logit, 0.0)
    votes_ref[...] = upward - downward


def norm_and_vote(pair_index, resid, gain, score, part_sum, prompts, cands):
    rows, width = resid.shape
    vmem = pl.BlockSpec(memory_space=pltpu.VMEM)
    return pl.pallas_call(
        norm_kernel,
        out_shape=(
            jax.ShapeDtypeStruct((rows, width), jnp.bfloat16),
            jax.ShapeDtypeStruct((cands, prompts), jnp.float32),
        ),
        in_specs=[pl.BlockSpec(memory_space=pltpu.SMEM)] + [vmem] * 4,
        out_specs=(vmem, vmem),
        cost_estimate=pl.CostEstimate(
            flops=rows * width * 8, bytes_accessed=2 << 20, transcendentals=rows
        ),
    )(pair_index, resid, gain, score, part_sum)


def together(*values):
    return lax.optimization_barrier(values)


def body(
    rank_query,
    rank_key,
    rank_value,
    rank_resid,
    out_weight,
    rank_gain,
    score_weight,
    pair_index,
    cand_rank,
    cand_len,
    blend_owner,
    blend_rows,
    blend_gain,
    blend_weight,
):
    local_heads = HR // NZ
    length = rank_query.shape[1]
    my_y, my_x, my_core, my_z = (lax.axis_index(a) for a in ("y", "x", "core", "z"))

    where = jnp.stack([my_y, my_x, my_core, my_z]).astype(jnp.int32)
    columns = lax.all_gather(out_weight.T, PLANE, axis=0, tiled=True)

    outgoing = select_rows(blend_owner, cand_rank, cand_len, blend_rows)
    rank_query, blend_weight, outgoing = together(rank_query, blend_weight, outgoing)
    prompts = blend_rows.shape[0]
    features = blend_rows.shape[3]
    arrived = lax.all_to_all(
        outgoing.reshape(prompts, -1, features), PLANE, split_axis=0, concat_axis=0, tiled=True
    )
    own = arrived.reshape(prompts * arrived.shape[1], features)

    context = pair_attention(rank_query, rank_key, rank_value, local_heads)
    depth = blend_weight.shape[0]
    slab = (my_y * NX + my_x) * NC + my_core
    gain = lax.dynamic_slice_in_dim(blend_gain, slab * depth, depth, 0).astype(jnp.float32)
    own_slab = (blend_weight.transpose(1, 0, 2).astype(jnp.float32) * gain[None, :, None]).astype(
        jnp.bfloat16
    )[None]
    gain_row = rank_gain.reshape(1, -1)
    score_row = score_weight.reshape(1, -1)
    own, context, own_slab, gain_row, score_row, where = together(
        own, context, own_slab, gain_row, score_row, where
    )

    lower = lax.ppermute(own, "z", ring(NZ, 1))
    upper = lax.ppermute(own, "z", ring(NZ, -1))
    x_before = lax.ppermute(own_slab, "x", ring(NX, 1))
    x_after = lax.ppermute(own_slab, "x", ring(NX, -1))
    x_across = lax.ppermute(x_before, "x", ring(NX, 1))
    strip = jnp.concatenate([own_slab, x_before, x_across, x_after], axis=0)
    lower, upper, strip, context = together(lower, upper, strip, context)
    blocks = {1: upper, NZ - 1: lower, 0: own}

    lower = lax.ppermute(lower, "z", ring(NZ, 1))
    upper = lax.ppermute(upper, "z", ring(NZ, -1))
    y_before = lax.ppermute(strip, "y", ring(NY, 1))
    y_after = lax.ppermute(strip, "y", ring(NY, -1))
    term_rows, token = project(context, columns)
    lower, upper, y_before, y_after, token = together(lower, upper, y_before, y_after, token)
    blocks.update({2: upper, NZ - 2: lower})
    part_sum = lax.psum_scatter(term_rows, "z", scatter_dimension=0, tiled=True)

    lower = lax.ppermute(lower, "z", ring(NZ, 1))
    upper = lax.ppermute(upper, "z", ring(NZ, -1))
    y_across = jnp.concatenate(
        [
            lax.ppermute(y_before[:2], "y", ring(NY, 1)),
            lax.ppermute(y_after[2:], "y", ring(NY, -1)),
        ],
        axis=0,
    )
    lower, upper, y_across = together(lower, upper, y_across)

    slabs = [strip, y_before, y_across, y_after]
    weights = arrange(where, token, slabs + [lax.ppermute(s, "core", ring(NC, 1)) for s in slabs])
    near = (0, 1, 2, NZ - 2, NZ - 1)
    half = own.shape[0] // 2
    total, squares = encode_first(near, [blocks[i] for i in near], weights)
    low = lax.ppermute(lower[:half], "z", ring(NZ, 1))
    high = lax.ppermute(upper[half:], "z", ring(NZ, -1))
    blended_qkv = encode_last(
        (3, NZ - 3, 4), upper, lower, low, high, weights, total, squares, prompts
    )

    part_sum, blended_qkv = together(part_sum, blended_qkv)
    own_pairs = rank_resid.shape[0]
    rank_hidden, votes = norm_and_vote(
        pair_index,
        rank_resid.reshape(own_pairs * length, -1),
        gain_row,
        score_row,
        part_sum,
        prompts,
        cand_rank.shape[1],
    )
    rank_hidden = rank_hidden.reshape(rank_resid.shape)
    votes = jnp.broadcast_to(votes[None], (NZ,) + votes.shape)
    votes = lax.all_to_all(votes, "z", split_axis=0, concat_axis=0, tiled=True)
    cand_score = jnp.sum(votes, axis=0).T
    return (rank_hidden, cand_score, blended_qkv)


def solution(mesh):
    grid = Mesh(mesh.devices.reshape(NY, NX, NC, NZ), ("y", "x", "core", "z"))
    whole = ("y", "x", "core", "z")
    placed = (
        P(PLANE, None, "z"),
        P(PLANE, None, "z"),
        P(PLANE, None, "z"),
        P(whole, None, None),
        P("z", PLANE),
        P(),
        P(),
        P(whole, None),
        P(PLANE, None),
        P(PLANE, None),
        P(PLANE, None),
        P(PLANE, None, None, "z"),
        P(),
        P(PLANE, None, "z"),
    )
    return jax.shard_map(
        body,
        mesh=grid,
        in_specs=placed,
        out_specs=(P(whole, None, None), P(PLANE, None), P(PLANE, None, None, "z")),
        check_vma=False,
    )
```

```python
import math

import jax
import jax.numpy as jnp
from jax import lax
from jax.experimental import pallas as pl
from jax.experimental.pallas import tpu as pltpu
from jax.sharding import Mesh, PartitionSpec as P

HR = 40
HDR = 128
NY, NX, NC, NZ = 4, 4, 2, 8
PLANE = ("y", "x", "core")


def ring(count, step):
    return [(i, (i + step) % count) for i in range(count)]


def pair_attention(queries, keys_in, values_in, head_count):
    pair_count, length, row_width = queries.shape
    head_size = row_width // head_count
    query_heads = queries.reshape(pair_count, length, head_count, head_size)
    key_heads = keys_in.reshape(pair_count, length, head_count, head_size)
    value_heads = values_in.reshape(pair_count, length, head_count, head_size)
    scores = jnp.einsum(
        "pihd,pjhd->phij", query_heads, key_heads, preferred_element_type=jnp.float32
    ) * (1.0 / math.sqrt(HDR))
    highest = jnp.max(scores, axis=-1, keepdims=True)
    weights = jnp.exp(scores - highest)
    soft_weights = (weights / jnp.sum(weights, axis=-1, keepdims=True)).astype(jnp.bfloat16)
    context = jnp.einsum(
        "phij,pjhd->pihd", soft_weights, value_heads, preferred_element_type=jnp.float32
    )
    return context.astype(jnp.bfloat16).reshape(pair_count * length, row_width)


def select_kernel(owner_ref, rank_ref, len_ref, rows_ref, out_ref, cand_ref, live_ref):
    places = rank_ref.shape[0]
    position = lax.broadcasted_iota(jnp.int32, rows_ref.shape[1:], 0)

    def one_prompt(prompt, carry):
        owner = owner_ref[0, prompt]
        for place in range(places):
            rank = rank_ref[place, prompt]
            cand_ref[prompt, rank] = place
            live_ref[prompt, rank] = len_ref[place, prompt]
        for rank in range(3):
            picked = rows_ref[prompt * places + cand_ref[prompt, rank]].astype(jnp.float32)
            chosen = jnp.where(position < live_ref[prompt, rank], picked, 0.0)
            out_ref[owner * 3 + rank] = chosen.astype(out_ref.dtype)
        return carry

    lax.fori_loop(0, owner_ref.shape[1], one_prompt, 0, unroll=4)


def select_rows(blend_owner, cand_rank, cand_len, blend_rows):
    prompts, cands, length, features = blend_rows.shape
    smem = pl.BlockSpec(memory_space=pltpu.SMEM)
    vmem = pl.BlockSpec(memory_space=pltpu.VMEM)
    return pl.pallas_call(
        select_kernel,
        out_shape=jax.ShapeDtypeStruct((prompts * 3, length, features), blend_rows.dtype),
        in_specs=[smem, smem, smem, vmem],
        out_specs=vmem,
        scratch_shapes=[pltpu.SMEM((prompts, cands), jnp.int32)] * 2,
        cost_estimate=pl.CostEstimate(flops=0, bytes_accessed=3 << 20, transcendentals=0),
    )(blend_owner, cand_rank.T, cand_len.T, blend_rows.reshape(prompts * cands, length, features))


def arrange_kernel(where_ref, token_ref, *refs):
    slab_refs, out_ref = refs[:-1], refs[-1]
    third, depth = slab_refs[0].shape[1:3]
    my_y, my_x, my_core, my_z = where_ref[0], where_ref[1], where_ref[2], where_ref[3]
    for swapped in range(NC):
        for back in range(NY):
            slabs = slab_refs[swapped * NY + back]
            for left in range(NX):
                slab_y = lax.rem(my_y - back + NY, NY)
                slab_x = lax.rem(my_x - left + NX, NX)
                slab_core = lax.rem(my_core + swapped, NC)
                slab = (slab_y * NX + slab_x) * NC + slab_core
                order = lax.rem(slab // 4 - my_z + NZ, NZ)
                start = pl.multiple_of((order * 4 + lax.rem(slab, 4)) * depth, depth)
                for part in range(third):
                    out_ref[part, pl.ds(start, depth), :] = slabs[left, part]


def arrange(where, token, slabs):
    third, depth, width = slabs[0].shape[1:]
    vmem = pl.BlockSpec(memory_space=pltpu.VMEM)
    return pl.pallas_call(
        arrange_kernel,
        out_shape=jax.ShapeDtypeStruct((third, NC * NY * NX * depth, width), jnp.bfloat16),
        in_specs=[pl.BlockSpec(memory_space=pltpu.SMEM)] + [vmem] * (len(slabs) + 1),
        out_specs=vmem,
        compiler_params=pltpu.CompilerParams(vmem_limit_bytes=32 << 20),
        cost_estimate=pl.CostEstimate(flops=0, bytes_accessed=12 << 20, transcendentals=0),
    )(where, token, *slabs)


def project_kernel(rows_ref, columns_ref, out_ref, token_ref):
    token_ref[...] = jnp.zeros_like(token_ref)
    out_ref[...] = lax.dot_general(
        rows_ref[...], columns_ref[...], (((1,), (1,)), ((), ())), preferred_element_type=jnp.float32
    ).astype(out_ref.dtype)


def project(rows, columns):
    count, depth = rows.shape
    width = columns.shape[0]
    steps = 4
    return pl.pallas_call(
        project_kernel,
        out_shape=(
            jax.ShapeDtypeStruct((count, width), jnp.bfloat16),
            jax.ShapeDtypeStruct((8, 128), jnp.float32),
        ),
        grid=(steps,),
        in_specs=[
            pl.BlockSpec((count, depth), lambda i: (0, 0)),
            pl.BlockSpec((width // steps, depth), lambda i: (i, 0)),
        ],
        out_specs=(
            pl.BlockSpec((count, width // steps), lambda i: (0, i)),
            pl.BlockSpec((8, 128), lambda i: (0, 0)),
        ),
        compiler_params=pltpu.CompilerParams(vmem_limit_bytes=16 << 20),
        cost_estimate=pl.CostEstimate(
            flops=2 * count * width * depth, bytes_accessed=9 << 20, transcendentals=0
        ),
    )(rows, columns)


def squares_of(values):
    value = values.astype(jnp.float32)
    return jnp.sum(value * value, axis=-1, keepdims=True)


def first_kernel(orders, *refs):
    row_refs = refs[: len(orders)]
    weight_ref, total_ref, squares_ref = refs[len(orders) :]
    features = row_refs[0].shape[1]
    squares = sum(squares_of(rows[...]) for rows in row_refs)
    squares_ref[...] = jnp.broadcast_to(squares, squares_ref.shape)
    for part in range(weight_ref.shape[0]):
        total_ref[part] = sum(
            jnp.dot(
                rows[...],
                weight_ref[part, order * features : (order + 1) * features, :],
                preferred_element_type=jnp.float32,
            )
            for order, rows in zip(orders, row_refs)
        )


def last_kernel(orders, row_a, row_b, low_ref, high_ref, weight_ref, total_ref, squares_ref, out_ref):
    features = row_a.shape[1]
    half_steps = pl.num_programs(0) // 2
    across = jnp.where(pl.program_id(0) < half_steps, low_ref[...], high_ref[...])
    values = [row_a[...], row_b[...], across]
    squares = squares_ref[:, :1] + sum(squares_of(value) for value in values)
    scale = lax.rsqrt(squares * (1.0 / (NZ * features)) + 1e-06)
    prompts, third, length, width = out_ref.shape
    for part in range(third):
        total = total_ref[part] + sum(
            jnp.dot(
                value,
                weight_ref[part, order * features : (order + 1) * features, :],
                preferred_element_type=jnp.float32,
            )
            for order, value in zip(orders, values)
        )
        out_ref[:, part] = (total * scale).astype(out_ref.dtype).reshape(prompts, length, width)


def whole_spec(array):
    return pl.BlockSpec(array.shape, lambda i: (0,) * array.ndim, pipeline_mode=pl.Buffered(1))


def encode_first(orders, blocks, weights):
    rows, features = blocks[0].shape
    third, _, width = weights.shape
    steps = 4
    step_rows = rows // steps
    return pl.pallas_call(
        lambda *refs: first_kernel(orders, *refs),
        out_shape=(
            jax.ShapeDtypeStruct((third, rows, width), jnp.float32),
            jax.ShapeDtypeStruct((rows, 128), jnp.float32),
        ),
        grid=(steps,),
        in_specs=[pl.BlockSpec((step_rows, features), lambda i: (i, 0))] * len(blocks)
        + [whole_spec(weights)],
        out_specs=(
            pl.BlockSpec((third, step_rows, width), lambda i: (0, i, 0)),
            pl.BlockSpec((step_rows, 128), lambda i: (i, 0)),
        ),
        compiler_params=pltpu.CompilerParams(vmem_limit_bytes=24 << 20),
        cost_estimate=pl.CostEstimate(
            flops=2 * rows * len(blocks) * features * third * width,
            bytes_accessed=12 << 20,
            transcendentals=0,
        ),
    )(*blocks, weights)


def encode_last(orders, row_a, row_b, low, high, weights, total, squares, prompts):
    rows, features = row_a.shape
    third, _, width = weights.shape
    length = rows // prompts
    steps = 4
    step_rows = rows // steps
    step_prompts = prompts // steps
    out = pl.pallas_call(
        lambda *refs: last_kernel(orders, *refs),
        out_shape=jax.ShapeDtypeStruct((prompts, third, length, width), jnp.bfloat16),
        grid=(steps,),
        in_specs=[
            pl.BlockSpec((step_rows, features), lambda i: (i, 0)),
            pl.BlockSpec((step_rows, features), lambda i: (i, 0)),
            pl.BlockSpec((step_rows, features), lambda i: (jnp.minimum(i, steps // 2 - 1), 0)),
            pl.BlockSpec((step_rows, features), lambda i: (jnp.maximum(i - steps // 2, 0), 0)),
            whole_spec(weights),
            pl.BlockSpec((third, step_rows, width), lambda i: (0, i, 0)),
            pl.BlockSpec((step_rows, 128), lambda i: (i, 0)),
        ],
        out_specs=pl.BlockSpec((step_prompts, third, length, width), lambda i: (i, 0, 0, 0)),
        compiler_params=pltpu.CompilerParams(vmem_limit_bytes=24 << 20),
        cost_estimate=pl.CostEstimate(
            flops=40 * rows * 3 * features * third * width,
            bytes_accessed=12 << 20,
            transcendentals=rows,
        ),
    )(row_a, row_b, low, high, weights, total, squares)
    return out.transpose(0, 2, 1, 3)


def normed_rows(resid_ref, gain_ref, sum_ref):
    mixed = resid_ref[...].astype(jnp.float32) + sum_ref[...].astype(jnp.float32)
    squares = jnp.sum(mixed * mixed, axis=-1, keepdims=True)
    scale = lax.rsqrt(squares * (1.0 / mixed.shape[1]) + 1e-05)
    return mixed * scale * gain_ref[...].astype(jnp.float32)


def norm_kernel(resid_ref, gain_ref, sum_ref, hidden_ref):
    hidden_ref[...] = normed_rows(resid_ref, gain_ref, sum_ref).astype(hidden_ref.dtype)


def vote_kernel(pair_ref, resid_ref, gain_ref, score_ref, sum_ref, votes_ref):
    normed = normed_rows(resid_ref, gain_ref, sum_ref)[:1]
    logit = jnp.sum(normed * score_ref[...].astype(jnp.float32), axis=-1, keepdims=True)
    cand = lax.broadcasted_iota(jnp.int32, votes_ref.shape, 0)
    prompt = lax.broadcasted_iota(jnp.int32, votes_ref.shape, 1)
    own = prompt == pair_ref[0, 0]
    upward = jnp.where(own & (cand == pair_ref[0, 1]), logit, 0.0)
    downward = jnp.where(own & (cand == pair_ref[0, 2]), logit, 0.0)
    votes_ref[...] = upward - downward


def norm(resid, gain, part_sum):
    rows, width = resid.shape
    vmem = pl.BlockSpec(memory_space=pltpu.VMEM)
    return pl.pallas_call(
        norm_kernel,
        out_shape=jax.ShapeDtypeStruct((rows, width), jnp.bfloat16),
        in_specs=[vmem] * 3,
        out_specs=vmem,
        cost_estimate=pl.CostEstimate(
            flops=rows * width * 8, bytes_accessed=2 << 20, transcendentals=rows
        ),
    )(resid, gain, part_sum)


def vote(pair_index, resid, gain, score, part_sum, prompts, cands):
    width = resid.shape[1]
    lead = pl.BlockSpec((16, width), lambda i: (0, 0))
    row = pl.BlockSpec((1, width), lambda i: (0, 0))
    return pl.pallas_call(
        vote_kernel,
        out_shape=jax.ShapeDtypeStruct((cands, prompts), jnp.float32),
        grid=(1,),
        in_specs=[pl.BlockSpec(memory_space=pltpu.SMEM), lead, row, row, lead],
        out_specs=pl.BlockSpec((cands, prompts), lambda i: (0, 0)),
        cost_estimate=pl.CostEstimate(
            flops=width * 128, bytes_accessed=1 << 18, transcendentals=16
        ),
    )(pair_index, resid, gain, score, part_sum)


def together(*values):
    return lax.optimization_barrier(values)


def body(
    rank_query,
    rank_key,
    rank_value,
    rank_resid,
    out_weight,
    rank_gain,
    score_weight,
    pair_index,
    cand_rank,
    cand_len,
    blend_owner,
    blend_rows,
    blend_gain,
    blend_weight,
):
    local_heads = HR // NZ
    length = rank_query.shape[1]
    my_y, my_x, my_core, my_z = (lax.axis_index(a) for a in ("y", "x", "core", "z"))

    where = jnp.stack([my_y, my_x, my_core, my_z]).astype(jnp.int32)
    columns = lax.all_gather(out_weight.T, PLANE, axis=0, tiled=True)

    outgoing = select_rows(blend_owner, cand_rank, cand_len, blend_rows)
    rank_query, blend_weight, outgoing = together(rank_query, blend_weight, outgoing)
    prompts = blend_rows.shape[0]
    features = blend_rows.shape[3]
    arrived = lax.all_to_all(
        outgoing.reshape(prompts, -1, features), PLANE, split_axis=0, concat_axis=0, tiled=True
    )
    own = arrived.reshape(prompts * arrived.shape[1], features)

    context = pair_attention(rank_query, rank_key, rank_value, local_heads)
    depth = blend_weight.shape[0]
    slab = (my_y * NX + my_x) * NC + my_core
    gain = lax.dynamic_slice_in_dim(blend_gain, slab * depth, depth, 0).astype(jnp.float32)
    own_slab = (blend_weight.transpose(1, 0, 2).astype(jnp.float32) * gain[None, :, None]).astype(
        jnp.bfloat16
    )[None]
    gain_row = rank_gain.reshape(1, -1)
    score_row = score_weight.reshape(1, -1)
    own, context, own_slab, gain_row, score_row, where = together(
        own, context, own_slab, gain_row, score_row, where
    )

    lower = lax.ppermute(own, "z", ring(NZ, 1))
    upper = lax.ppermute(own, "z", ring(NZ, -1))
    x_before = lax.ppermute(own_slab, "x", ring(NX, 1))
    x_after = lax.ppermute(own_slab, "x", ring(NX, -1))
    x_across = lax.ppermute(x_before, "x", ring(NX, 1))
    strip = jnp.concatenate([own_slab, x_before, x_across, x_after], axis=0)
    lower, upper, strip = together(lower, upper, strip)
    blocks = {1: upper, NZ - 1: lower, 0: own}

    lower = lax.ppermute(lower, "z", ring(NZ, 1))
    upper = lax.ppermute(upper, "z", ring(NZ, -1))
    y_before = lax.ppermute(strip, "y", ring(NY, 1))
    y_after = lax.ppermute(strip, "y", ring(NY, -1))
    lower, upper, y_before, y_after, context = together(lower, upper, y_before, y_after, context)
    blocks.update({2: upper, NZ - 2: lower})
    term_rows, token = project(context, columns)
    part_sum = lax.psum_scatter(term_rows, "z", scatter_dimension=0, tiled=True)

    lower = lax.ppermute(lower, "z", ring(NZ, 1))
    upper = lax.ppermute(upper, "z", ring(NZ, -1))
    y_across = jnp.concatenate(
        [
            lax.ppermute(y_before[:2], "y", ring(NY, 1)),
            lax.ppermute(y_after[2:], "y", ring(NY, -1)),
        ],
        axis=0,
    )
    lower, upper, y_across, token = together(lower, upper, y_across, token)

    slabs = [strip, y_before, y_across, y_after]
    weights = arrange(where, token, slabs + [lax.ppermute(s, "core", ring(NC, 1)) for s in slabs])
    near = (0, 1, 2, NZ - 2, NZ - 1)
    half = own.shape[0] // 2
    total, squares = encode_first(near, [blocks[i] for i in near], weights)
    low = lax.ppermute(lower[:half], "z", ring(NZ, 1))
    high = lax.ppermute(upper[half:], "z", ring(NZ, -1))
    blended_qkv = encode_last(
        (3, NZ - 3, 4), upper, lower, low, high, weights, total, squares, prompts
    )

    part_sum, blended_qkv = together(part_sum, blended_qkv)
    own_pairs = rank_resid.shape[0]
    resid = rank_resid.reshape(own_pairs * length, -1)
    votes = vote(
        pair_index, resid, gain_row, score_row, part_sum, prompts, cand_rank.shape[1]
    )
    shifts = [[(i, i // 4 * 4 + (i + step) % 4) for i in range(NZ)] for step in (1, 2, 3)]
    votes = votes + sum([lax.ppermute(votes, "z", shift) for shift in shifts])
    votes = votes + lax.ppermute(votes, "z", ring(NZ, NZ // 2))
    cand_score = votes.T
    rank_hidden = norm(resid, gain_row, part_sum).reshape(rank_resid.shape)
    return (rank_hidden, cand_score, blended_qkv)


def solution(mesh):
    grid = Mesh(mesh.devices.reshape(NY, NX, NC, NZ), ("y", "x", "core", "z"))
    whole = ("y", "x", "core", "z")
    placed = (
        P(PLANE, None, "z"),
        P(PLANE, None, "z"),
        P(PLANE, None, "z"),
        P(whole, None, None),
        P("z", PLANE),
        P(),
        P(),
        P(whole, None),
        P(PLANE, None),
        P(PLANE, None),
        P(PLANE, None),
        P(PLANE, None, None, "z"),
        P(),
        P(PLANE, None, "z"),
    )
    return jax.shard_map(
        body,
        mesh=grid,
        in_specs=placed,
        out_specs=(P(whole, None, None), P(PLANE, None), P(PLANE, None, None, "z")),
        check_vma=False,
    )
```

```python
import math

import jax
import jax.numpy as jnp
from jax import lax
from jax.experimental import pallas as pl
from jax.experimental.pallas import tpu as pltpu
from jax.sharding import Mesh, PartitionSpec as P

HR = 40
HDR = 128
NY, NX, NC, NZ = 4, 4, 2, 8
PLANE = ("y", "x", "core")


def ring(count, step):
    return [(i, (i + step) % count) for i in range(count)]


def pair_attention(queries, keys_in, values_in, head_count):
    pair_count, length, row_width = queries.shape
    head_size = row_width // head_count
    query_heads = queries.reshape(pair_count, length, head_count, head_size)
    key_heads = keys_in.reshape(pair_count, length, head_count, head_size)
    value_heads = values_in.reshape(pair_count, length, head_count, head_size)
    scores = jnp.einsum(
        "pihd,pjhd->phij", query_heads, key_heads, preferred_element_type=jnp.float32
    ) * (1.0 / math.sqrt(HDR))
    highest = jnp.max(scores, axis=-1, keepdims=True)
    weights = jnp.exp(scores - highest)
    soft_weights = (weights / jnp.sum(weights, axis=-1, keepdims=True)).astype(jnp.bfloat16)
    context = jnp.einsum(
        "phij,pjhd->pihd", soft_weights, value_heads, preferred_element_type=jnp.float32
    )
    return context.astype(jnp.bfloat16).reshape(pair_count * length, row_width)


def select_kernel(owner_ref, rank_ref, len_ref, rows_ref, out_ref, cand_ref, live_ref):
    places = rank_ref.shape[0]
    position = lax.broadcasted_iota(jnp.int32, rows_ref.shape[1:], 0)

    def one_prompt(prompt, carry):
        owner = owner_ref[0, prompt]
        for place in range(places):
            rank = rank_ref[place, prompt]
            cand_ref[prompt, rank] = place
            live_ref[prompt, rank] = len_ref[place, prompt]
        for rank in range(3):
            picked = rows_ref[prompt * places + cand_ref[prompt, rank]].astype(jnp.float32)
            chosen = jnp.where(position < live_ref[prompt, rank], picked, 0.0)
            out_ref[owner * 3 + rank] = chosen.astype(out_ref.dtype)
        return carry

    lax.fori_loop(0, owner_ref.shape[1], one_prompt, 0, unroll=4)


def select_rows(blend_owner, cand_rank, cand_len, blend_rows):
    prompts, cands, length, features = blend_rows.shape
    smem = pl.BlockSpec(memory_space=pltpu.SMEM)
    vmem = pl.BlockSpec(memory_space=pltpu.VMEM)
    return pl.pallas_call(
        select_kernel,
        out_shape=jax.ShapeDtypeStruct((prompts * 3, length, features), blend_rows.dtype),
        in_specs=[smem, smem, smem, vmem],
        out_specs=vmem,
        scratch_shapes=[pltpu.SMEM((prompts, cands), jnp.int32)] * 2,
        cost_estimate=pl.CostEstimate(flops=0, bytes_accessed=3 << 20, transcendentals=0),
    )(blend_owner, cand_rank.T, cand_len.T, blend_rows.reshape(prompts * cands, length, features))


def arrange_kernel(where_ref, token_ref, *refs):
    slab_refs, out_ref = refs[:-1], refs[-1]
    third, depth = slab_refs[0].shape[1:3]
    my_y, my_x, my_core, my_z = where_ref[0], where_ref[1], where_ref[2], where_ref[3]
    for swapped in range(NC):
        for back in range(NY):
            slabs = slab_refs[swapped * NY + back]
            for left in range(NX):
                slab_y = lax.rem(my_y - back + NY, NY)
                slab_x = lax.rem(my_x - left + NX, NX)
                slab_core = lax.rem(my_core + swapped, NC)
                slab = (slab_y * NX + slab_x) * NC + slab_core
                order = lax.rem(slab // 4 - my_z + NZ, NZ)
                start = pl.multiple_of((order * 4 + lax.rem(slab, 4)) * depth, depth)
                for part in range(third):
                    out_ref[part, pl.ds(start, depth), :] = slabs[left, part]


def arrange(where, token, slabs):
    third, depth, width = slabs[0].shape[1:]
    vmem = pl.BlockSpec(memory_space=pltpu.VMEM)
    return pl.pallas_call(
        arrange_kernel,
        out_shape=jax.ShapeDtypeStruct((third, NC * NY * NX * depth, width), jnp.bfloat16),
        in_specs=[pl.BlockSpec(memory_space=pltpu.SMEM)] + [vmem] * (len(slabs) + 1),
        out_specs=vmem,
        compiler_params=pltpu.CompilerParams(vmem_limit_bytes=32 << 20),
        cost_estimate=pl.CostEstimate(flops=0, bytes_accessed=12 << 20, transcendentals=0),
    )(where, token, *slabs)


def project_kernel(rows_ref, columns_ref, out_ref, token_ref):
    token_ref[...] = jnp.zeros_like(token_ref)
    out_ref[...] = lax.dot_general(
        rows_ref[...], columns_ref[...], (((1,), (1,)), ((), ())), preferred_element_type=jnp.float32
    ).astype(out_ref.dtype)


def project(rows, columns):
    count, depth = rows.shape
    width = columns.shape[0]
    steps = 4
    return pl.pallas_call(
        project_kernel,
        out_shape=(
            jax.ShapeDtypeStruct((count, width), jnp.bfloat16),
            jax.ShapeDtypeStruct((8, 128), jnp.float32),
        ),
        grid=(steps,),
        in_specs=[
            pl.BlockSpec((count, depth), lambda i: (0, 0)),
            pl.BlockSpec((width // steps, depth), lambda i: (i, 0)),
        ],
        out_specs=(
            pl.BlockSpec((count, width // steps), lambda i: (0, i)),
            pl.BlockSpec((8, 128), lambda i: (0, 0)),
        ),
        compiler_params=pltpu.CompilerParams(vmem_limit_bytes=16 << 20),
        cost_estimate=pl.CostEstimate(
            flops=2 * count * width * depth, bytes_accessed=9 << 20, transcendentals=0
        ),
    )(rows, columns)


def squares_of(values):
    value = values.astype(jnp.float32)
    return jnp.sum(value * value, axis=-1, keepdims=True)


def first_kernel(orders, *refs):
    row_refs = refs[: len(orders)]
    weight_ref, total_ref, squares_ref = refs[len(orders) :]
    features = row_refs[0].shape[1]
    squares = sum(squares_of(rows[...]) for rows in row_refs)
    squares_ref[...] = jnp.broadcast_to(squares, squares_ref.shape)
    for part in range(weight_ref.shape[0]):
        total_ref[part] = sum(
            jnp.dot(
                rows[...],
                weight_ref[part, order * features : (order + 1) * features, :],
                preferred_element_type=jnp.float32,
            )
            for order, rows in zip(orders, row_refs)
        )


def last_kernel(orders, row_a, row_b, low_ref, high_ref, weight_ref, total_ref, squares_ref, out_ref):
    features = row_a.shape[1]
    half_steps = pl.num_programs(0) // 2
    across = jnp.where(pl.program_id(0) < half_steps, low_ref[...], high_ref[...])
    values = [row_a[...], row_b[...], across]
    squares = squares_ref[:, :1] + sum(squares_of(value) for value in values)
    scale = lax.rsqrt(squares * (1.0 / (NZ * features)) + 1e-06)
    prompts, third, length, width = out_ref.shape
    for part in range(third):
        total = total_ref[part] + sum(
            jnp.dot(
                value,
                weight_ref[part, order * features : (order + 1) * features, :],
                preferred_element_type=jnp.float32,
            )
            for order, value in zip(orders, values)
        )
        out_ref[:, part] = (total * scale).astype(out_ref.dtype).reshape(prompts, length, width)


def whole_spec(array):
    return pl.BlockSpec(array.shape, lambda i: (0,) * array.ndim, pipeline_mode=pl.Buffered(1))


def encode_first(orders, blocks, weights):
    rows, features = blocks[0].shape
    third, _, width = weights.shape
    steps = 4
    step_rows = rows // steps
    return pl.pallas_call(
        lambda *refs: first_kernel(orders, *refs),
        out_shape=(
            jax.ShapeDtypeStruct((third, rows, width), jnp.float32),
            jax.ShapeDtypeStruct((rows, 128), jnp.float32),
        ),
        grid=(steps,),
        in_specs=[pl.BlockSpec((step_rows, features), lambda i: (i, 0))] * len(blocks)
        + [whole_spec(weights)],
        out_specs=(
            pl.BlockSpec((third, step_rows, width), lambda i: (0, i, 0)),
            pl.BlockSpec((step_rows, 128), lambda i: (i, 0)),
        ),
        compiler_params=pltpu.CompilerParams(vmem_limit_bytes=24 << 20),
        cost_estimate=pl.CostEstimate(
            flops=2 * rows * len(blocks) * features * third * width,
            bytes_accessed=12 << 20,
            transcendentals=0,
        ),
    )(*blocks, weights)


def encode_last(orders, row_a, row_b, low, high, weights, total, squares, prompts):
    rows, features = row_a.shape
    third, _, width = weights.shape
    length = rows // prompts
    steps = 4
    step_rows = rows // steps
    step_prompts = prompts // steps
    out = pl.pallas_call(
        lambda *refs: last_kernel(orders, *refs),
        out_shape=jax.ShapeDtypeStruct((prompts, third, length, width), jnp.bfloat16),
        grid=(steps,),
        in_specs=[
            pl.BlockSpec((step_rows, features), lambda i: (i, 0)),
            pl.BlockSpec((step_rows, features), lambda i: (i, 0)),
            pl.BlockSpec((step_rows, features), lambda i: (jnp.minimum(i, steps // 2 - 1), 0)),
            pl.BlockSpec((step_rows, features), lambda i: (jnp.maximum(i - steps // 2, 0), 0)),
            whole_spec(weights),
            pl.BlockSpec((third, step_rows, width), lambda i: (0, i, 0)),
            pl.BlockSpec((step_rows, 128), lambda i: (i, 0)),
        ],
        out_specs=pl.BlockSpec((step_prompts, third, length, width), lambda i: (i, 0, 0, 0)),
        compiler_params=pltpu.CompilerParams(vmem_limit_bytes=24 << 20),
        cost_estimate=pl.CostEstimate(
            flops=40 * rows * 3 * features * third * width,
            bytes_accessed=12 << 20,
            transcendentals=rows,
        ),
    )(row_a, row_b, low, high, weights, total, squares)
    return out.transpose(0, 2, 1, 3)


def norm_kernel(pair_ref, resid_ref, gain_ref, score_ref, sum_ref, hidden_ref, votes_ref):
    mixed = resid_ref[...].astype(jnp.float32) + sum_ref[...].astype(jnp.float32)
    squares = jnp.sum(mixed * mixed, axis=-1, keepdims=True)
    scale = lax.rsqrt(squares * (1.0 / mixed.shape[1]) + 1e-05)
    normed = mixed * scale * gain_ref[...].astype(jnp.float32)
    hidden_ref[...] = normed.astype(hidden_ref.dtype)
    logit = jnp.sum(normed[:1] * score_ref[...].astype(jnp.float32), axis=-1, keepdims=True)
    cand = lax.broadcasted_iota(jnp.int32, votes_ref.shape, 0)
    prompt = lax.broadcasted_iota(jnp.int32, votes_ref.shape, 1)
    own = prompt == pair_ref[0, 0]
    upward = jnp.where(own & (cand == pair_ref[0, 1]), logit, 0.0)
    downward = jnp.where(own & (cand == pair_ref[0, 2]), logit, 0.0)
    votes_ref[...] = upward - downward


def norm_and_vote(pair_index, resid, gain, score, part_sum, prompts, cands):
    rows, width = resid.shape
    vmem = pl.BlockSpec(memory_space=pltpu.VMEM)
    return pl.pallas_call(
        norm_kernel,
        out_shape=(
            jax.ShapeDtypeStruct((rows, width), jnp.bfloat16),
            jax.ShapeDtypeStruct((cands, prompts), jnp.float32),
        ),
        in_specs=[pl.BlockSpec(memory_space=pltpu.SMEM)] + [vmem] * 4,
        out_specs=(vmem, vmem),
        cost_estimate=pl.CostEstimate(
            flops=rows * width * 8, bytes_accessed=2 << 20, transcendentals=rows
        ),
    )(pair_index, resid, gain, score, part_sum)


def together(*values):
    return lax.optimization_barrier(values)


def body(
    rank_query,
    rank_key,
    rank_value,
    rank_resid,
    out_weight,
    rank_gain,
    score_weight,
    pair_index,
    cand_rank,
    cand_len,
    blend_owner,
    blend_rows,
    blend_gain,
    blend_weight,
):
    local_heads = HR // NZ
    length = rank_query.shape[1]
    my_y, my_x, my_core, my_z = (lax.axis_index(a) for a in ("y", "x", "core", "z"))

    where = jnp.stack([my_y, my_x, my_core, my_z]).astype(jnp.int32)
    columns = lax.all_gather(out_weight.T, PLANE, axis=0, tiled=True)

    outgoing = select_rows(blend_owner, cand_rank, cand_len, blend_rows)
    rank_query, blend_weight, outgoing = together(rank_query, blend_weight, outgoing)
    prompts = blend_rows.shape[0]
    features = blend_rows.shape[3]
    arrived = lax.all_to_all(
        outgoing.reshape(prompts, -1, features), PLANE, split_axis=0, concat_axis=0, tiled=True
    )
    own = arrived.reshape(prompts * arrived.shape[1], features)

    context = pair_attention(rank_query, rank_key, rank_value, local_heads)
    depth = blend_weight.shape[0]
    slab = (my_y * NX + my_x) * NC + my_core
    gain = lax.dynamic_slice_in_dim(blend_gain, slab * depth, depth, 0).astype(jnp.float32)
    own_slab = (blend_weight.transpose(1, 0, 2).astype(jnp.float32) * gain[None, :, None]).astype(
        jnp.bfloat16
    )[None]
    gain_row = rank_gain.reshape(1, -1)
    score_row = score_weight.reshape(1, -1)
    own, context, own_slab, gain_row, score_row, where = together(
        own, context, own_slab, gain_row, score_row, where
    )

    lower = lax.ppermute(own, "z", ring(NZ, 1))
    upper = lax.ppermute(own, "z", ring(NZ, -1))
    x_before = lax.ppermute(own_slab, "x", ring(NX, 1))
    x_after = lax.ppermute(own_slab, "x", ring(NX, -1))
    x_across = lax.ppermute(x_before, "x", ring(NX, 1))
    strip = jnp.concatenate([own_slab, x_before, x_across, x_after], axis=0)
    lower, upper, strip, context = together(lower, upper, strip, context)
    blocks = {1: upper, NZ - 1: lower, 0: own}

    lower = lax.ppermute(lower, "z", ring(NZ, 1))
    upper = lax.ppermute(upper, "z", ring(NZ, -1))
    y_before = lax.ppermute(strip, "y", ring(NY, 1))
    y_after = lax.ppermute(strip, "y", ring(NY, -1))
    term_rows, token = project(context, columns)
    lower, upper, token = together(lower, upper, token)
    blocks.update({2: upper, NZ - 2: lower})
    part_sum = lax.psum_scatter(term_rows, "z", scatter_dimension=0, tiled=True)

    lower = lax.ppermute(lower, "z", ring(NZ, 1))
    upper = lax.ppermute(upper, "z", ring(NZ, -1))
    y_across = jnp.concatenate(
        [
            lax.ppermute(y_before[:2], "y", ring(NY, 1)),
            lax.ppermute(y_after[2:], "y", ring(NY, -1)),
        ],
        axis=0,
    )
    lower, upper, y_across = together(lower, upper, y_across)

    slabs = [strip, y_before, y_across, y_after]
    weights = arrange(where, token, slabs + [lax.ppermute(s, "core", ring(NC, 1)) for s in slabs])
    near = (0, 1, 2, NZ - 2, NZ - 1)
    half = own.shape[0] // 2
    total, squares = encode_first(near, [blocks[i] for i in near], weights)
    low = lax.ppermute(lower[:half], "z", ring(NZ, 1))
    high = lax.ppermute(upper[half:], "z", ring(NZ, -1))
    blended_qkv = encode_last(
        (3, NZ - 3, 4), upper, lower, low, high, weights, total, squares, prompts
    )

    part_sum, blended_qkv = together(part_sum, blended_qkv)
    own_pairs = rank_resid.shape[0]
    rank_hidden, votes = norm_and_vote(
        pair_index,
        rank_resid.reshape(own_pairs * length, -1),
        gain_row,
        score_row,
        part_sum,
        prompts,
        cand_rank.shape[1],
    )
    rank_hidden = rank_hidden.reshape(rank_resid.shape)
    votes = jnp.broadcast_to(votes[None], (NZ,) + votes.shape)
    votes = lax.all_to_all(votes, "z", split_axis=0, concat_axis=0, tiled=True)
    cand_score = jnp.sum(votes, axis=0).T
    return (rank_hidden, cand_score, blended_qkv)


def solution(mesh):
    grid = Mesh(mesh.devices.reshape(NY, NX, NC, NZ), ("y", "x", "core", "z"))
    whole = ("y", "x", "core", "z")
    placed = (
        P(PLANE, None, "z"),
        P(PLANE, None, "z"),
        P(PLANE, None, "z"),
        P(whole, None, None),
        P("z", PLANE),
        P(),
        P(),
        P(whole, None),
        P(PLANE, None),
        P(PLANE, None),
        P(PLANE, None),
        P(PLANE, None, None, "z"),
        P(),
        P(PLANE, None, "z"),
    )
    return jax.shard_map(
        body,
        mesh=grid,
        in_specs=placed,
        out_specs=(P(whole, None, None), P(PLANE, None), P(PLANE, None, None, "z")),
        check_vma=False,
    )
```

```python
import math

import jax
import jax.numpy as jnp
from jax import lax
from jax.experimental import pallas as pl
from jax.experimental.pallas import tpu as pltpu
from jax.sharding import Mesh, PartitionSpec as P

HR = 40
HDR = 128
NY, NX, NC, NZ = 4, 4, 2, 8
PLANE = ("y", "x", "core")


def ring(count, step):
    return [(i, (i + step) % count) for i in range(count)]


def pair_attention(queries, keys_in, values_in, head_count):
    pair_count, length, row_width = queries.shape
    head_size = row_width // head_count
    query_heads = queries.reshape(pair_count, length, head_count, head_size)
    key_heads = keys_in.reshape(pair_count, length, head_count, head_size)
    value_heads = values_in.reshape(pair_count, length, head_count, head_size)
    scores = jnp.einsum(
        "pihd,pjhd->phij", query_heads, key_heads, preferred_element_type=jnp.float32
    ) * (1.0 / math.sqrt(HDR))
    highest = jnp.max(scores, axis=-1, keepdims=True)
    weights = jnp.exp(scores - highest)
    soft_weights = (weights / jnp.sum(weights, axis=-1, keepdims=True)).astype(jnp.bfloat16)
    context = jnp.einsum(
        "phij,pjhd->pihd", soft_weights, value_heads, preferred_element_type=jnp.float32
    )
    return context.astype(jnp.bfloat16).reshape(pair_count * length, row_width)


def select_kernel(owner_ref, rank_ref, len_ref, rows_ref, out_ref, cand_ref, live_ref):
    places = rank_ref.shape[0]
    position = lax.broadcasted_iota(jnp.int32, rows_ref.shape[1:], 0)

    def one_prompt(prompt, carry):
        owner = owner_ref[0, prompt]
        for place in range(places):
            rank = rank_ref[place, prompt]
            cand_ref[prompt, rank] = place
            live_ref[prompt, rank] = len_ref[place, prompt]
        for rank in range(3):
            picked = rows_ref[prompt * places + cand_ref[prompt, rank]].astype(jnp.float32)
            chosen = jnp.where(position < live_ref[prompt, rank], picked, 0.0)
            out_ref[owner * 3 + rank] = chosen.astype(out_ref.dtype)
        return carry

    lax.fori_loop(0, owner_ref.shape[1], one_prompt, 0, unroll=4)


def select_rows(blend_owner, cand_rank, cand_len, blend_rows):
    prompts, cands, length, features = blend_rows.shape
    smem = pl.BlockSpec(memory_space=pltpu.SMEM)
    vmem = pl.BlockSpec(memory_space=pltpu.VMEM)
    return pl.pallas_call(
        select_kernel,
        out_shape=jax.ShapeDtypeStruct((prompts * 3, length, features), blend_rows.dtype),
        in_specs=[smem, smem, smem, vmem],
        out_specs=vmem,
        scratch_shapes=[pltpu.SMEM((prompts, cands), jnp.int32)] * 2,
        cost_estimate=pl.CostEstimate(flops=0, bytes_accessed=3 << 20, transcendentals=0),
    )(blend_owner, cand_rank.T, cand_len.T, blend_rows.reshape(prompts * cands, length, features))


def arrange_kernel(where_ref, token_ref, *refs):
    slab_refs, out_ref = refs[:-1], refs[-1]
    third, depth = slab_refs[0].shape[1:3]
    my_y, my_x, my_core, my_z = where_ref[0], where_ref[1], where_ref[2], where_ref[3]
    for swapped in range(NC):
        for back in range(NY):
            slabs = slab_refs[swapped * NY + back]
            for left in range(NX):
                slab_y = lax.rem(my_y - back + NY, NY)
                slab_x = lax.rem(my_x - left + NX, NX)
                slab_core = lax.rem(my_core + swapped, NC)
                slab = (slab_y * NX + slab_x) * NC + slab_core
                order = lax.rem(slab // 4 - my_z + NZ, NZ)
                start = pl.multiple_of((order * 4 + lax.rem(slab, 4)) * depth, depth)
                for part in range(third):
                    out_ref[part, pl.ds(start, depth), :] = slabs[left, part]


def arrange(where, token, slabs):
    third, depth, width = slabs[0].shape[1:]
    vmem = pl.BlockSpec(memory_space=pltpu.VMEM)
    return pl.pallas_call(
        arrange_kernel,
        out_shape=jax.ShapeDtypeStruct((third, NC * NY * NX * depth, width), jnp.bfloat16),
        in_specs=[pl.BlockSpec(memory_space=pltpu.SMEM)] + [vmem] * (len(slabs) + 1),
        out_specs=vmem,
        compiler_params=pltpu.CompilerParams(vmem_limit_bytes=32 << 20),
        cost_estimate=pl.CostEstimate(flops=0, bytes_accessed=12 << 20, transcendentals=0),
    )(where, token, *slabs)


def project_kernel(own_ref, before_ref, low_ref, high_ref, after_ref, columns_ref, out_ref, token_ref):
    def project(rows):
        pairs, length, depth = rows.shape
        product = lax.dot_general(
            rows.reshape(pairs * length, depth),
            columns_ref[...],
            (((1,), (1,)), ((), ())),
            preferred_element_type=jnp.float32,
        )
        return product.astype(out_ref.dtype).reshape(pairs, length, -1)

    token_ref[...] = jnp.zeros_like(token_ref)
    half = low_ref.shape[0]
    out_ref[:, 0] = project(own_ref[...])
    out_ref[:, 1] = project(before_ref[...])
    out_ref[:half, 2] = project(low_ref[...])
    out_ref[half:, 2] = project(high_ref[...])
    out_ref[:, 3] = project(after_ref[...])


def project(contexts, columns):
    pairs, length, depth = contexts[0].shape
    width = columns.shape[0]
    vmem = pl.BlockSpec(memory_space=pltpu.VMEM)
    return pl.pallas_call(
        project_kernel,
        out_shape=(
            jax.ShapeDtypeStruct((pairs, NY, length, width), jnp.bfloat16),
            jax.ShapeDtypeStruct((8, 128), jnp.float32),
        ),
        in_specs=[vmem] * (len(contexts) + 1),
        out_specs=(vmem, vmem),
        compiler_params=pltpu.CompilerParams(vmem_limit_bytes=20 << 20),
        cost_estimate=pl.CostEstimate(
            flops=2 * pairs * NY * length * width * depth, bytes_accessed=6 << 20, transcendentals=0
        ),
    )(*contexts, columns)


def squares_of(values):
    value = values.astype(jnp.float32)
    return jnp.sum(value * value, axis=-1, keepdims=True)


def first_kernel(orders, *refs):
    row_refs = refs[: len(orders)]
    weight_ref, total_ref, squares_ref = refs[len(orders) :]
    features = row_refs[0].shape[1]
    squares = sum(squares_of(rows[...]) for rows in row_refs)
    squares_ref[...] = jnp.broadcast_to(squares, squares_ref.shape)
    for part in range(weight_ref.shape[0]):
        total_ref[part] = sum(
            jnp.dot(
                rows[...],
                weight_ref[part, order * features : (order + 1) * features, :],
                preferred_element_type=jnp.float32,
            )
            for order, rows in zip(orders, row_refs)
        )


def last_kernel(orders, row_a, row_b, low_ref, high_ref, weight_ref, total_ref, squares_ref, out_ref):
    features = row_a.shape[1]
    half_steps = pl.num_programs(0) // 2
    across = jnp.where(pl.program_id(0) < half_steps, low_ref[...], high_ref[...])
    values = [row_a[...], row_b[...], across]
    squares = squares_ref[:, :1] + sum(squares_of(value) for value in values)
    scale = lax.rsqrt(squares * (1.0 / (NZ * features)) + 1e-06)
    prompts, third, length, width = out_ref.shape
    for part in range(third):
        total = total_ref[part] + sum(
            jnp.dot(
                value,
                weight_ref[part, order * features : (order + 1) * features, :],
                preferred_element_type=jnp.float32,
            )
            for order, value in zip(orders, values)
        )
        out_ref[:, part] = (total * scale).astype(out_ref.dtype).reshape(prompts, length, width)


def whole_spec(array):
    return pl.BlockSpec(array.shape, lambda i: (0,) * array.ndim, pipeline_mode=pl.Buffered(1))


def encode_first(orders, blocks, weights):
    rows, features = blocks[0].shape
    third, _, width = weights.shape
    steps = 4
    step_rows = rows // steps
    return pl.pallas_call(
        lambda *refs: first_kernel(orders, *refs),
        out_shape=(
            jax.ShapeDtypeStruct((third, rows, width), jnp.float32),
            jax.ShapeDtypeStruct((rows, 128), jnp.float32),
        ),
        grid=(steps,),
        in_specs=[pl.BlockSpec((step_rows, features), lambda i: (i, 0))] * len(blocks)
        + [whole_spec(weights)],
        out_specs=(
            pl.BlockSpec((third, step_rows, width), lambda i: (0, i, 0)),
            pl.BlockSpec((step_rows, 128), lambda i: (i, 0)),
        ),
        compiler_params=pltpu.CompilerParams(vmem_limit_bytes=24 << 20),
        cost_estimate=pl.CostEstimate(
            flops=2 * rows * len(blocks) * features * third * width,
            bytes_accessed=12 << 20,
            transcendentals=0,
        ),
    )(*blocks, weights)


def encode_last(orders, row_a, row_b, low, high, weights, total, squares, prompts):
    rows, features = row_a.shape
    third, _, width = weights.shape
    length = rows // prompts
    steps = 4
    step_rows = rows // steps
    step_prompts = prompts // steps
    out = pl.pallas_call(
        lambda *refs: last_kernel(orders, *refs),
        out_shape=jax.ShapeDtypeStruct((prompts, third, length, width), jnp.bfloat16),
        grid=(steps,),
        in_specs=[
            pl.BlockSpec((step_rows, features), lambda i: (i, 0)),
            pl.BlockSpec((step_rows, features), lambda i: (i, 0)),
            pl.BlockSpec((step_rows, features), lambda i: (jnp.minimum(i, steps // 2 - 1), 0)),
            pl.BlockSpec((step_rows, features), lambda i: (jnp.maximum(i - steps // 2, 0), 0)),
            whole_spec(weights),
            pl.BlockSpec((third, step_rows, width), lambda i: (0, i, 0)),
            pl.BlockSpec((step_rows, 128), lambda i: (i, 0)),
        ],
        out_specs=pl.BlockSpec((step_prompts, third, length, width), lambda i: (i, 0, 0, 0)),
        compiler_params=pltpu.CompilerParams(vmem_limit_bytes=24 << 20),
        cost_estimate=pl.CostEstimate(
            flops=40 * rows * 3 * features * third * width,
            bytes_accessed=12 << 20,
            transcendentals=rows,
        ),
    )(row_a, row_b, low, high, weights, total, squares)
    return out.transpose(0, 2, 1, 3)


def norm_kernel(where_ref, pair_ref, resid_ref, gain_ref, score_ref, *refs):
    piece_refs = refs[:NY]
    hidden_ref, votes_ref, mixed_ref = refs[NY:]
    rows, quarter = piece_refs[0].shape
    squares = jnp.zeros((rows, 1), jnp.float32)
    for ahead, piece in enumerate(piece_refs):
        place = lax.rem(where_ref[0] + ahead, NY)
        columns = pl.ds(pl.multiple_of(place * quarter, 128), quarter)
        mixed = resid_ref[:, columns].astype(jnp.float32) + piece[...].astype(jnp.float32)
        mixed_ref[:, columns] = mixed
        squares = squares + jnp.sum(mixed * mixed, axis=-1, keepdims=True)
    scale = lax.rsqrt(squares * (1.0 / (NY * quarter)) + 1e-05)
    normed = mixed_ref[...] * scale * gain_ref[...].astype(jnp.float32)
    hidden_ref[...] = normed.astype(hidden_ref.dtype)
    logit = jnp.sum(
        normed[:1] * score_ref[...].astype(jnp.float32), axis=-1, keepdims=True
    )
    cand = lax.broadcasted_iota(jnp.int32, votes_ref.shape, 0)
    prompt = lax.broadcasted_iota(jnp.int32, votes_ref.shape, 1)
    own = prompt == pair_ref[0, 0]
    upward = jnp.where(own & (cand == pair_ref[0, 1]), logit, 0.0)
    downward = jnp.where(own & (cand == pair_ref[0, 2]), logit, 0.0)
    votes_ref[...] = upward - downward


def norm_and_vote(where, pair_index, resid, gain, score, pieces, prompts, cands):
    rows, width = resid.shape
    smem = pl.BlockSpec(memory_space=pltpu.SMEM)
    vmem = pl.BlockSpec(memory_space=pltpu.VMEM)
    return pl.pallas_call(
        norm_kernel,
        out_shape=(
            jax.ShapeDtypeStruct((rows, width), jnp.bfloat16),
            jax.ShapeDtypeStruct((cands, prompts), jnp.float32),
        ),
        in_specs=[smem, smem] + [vmem] * (3 + NY),
        out_specs=(vmem, vmem),
        scratch_shapes=[pltpu.VMEM((rows, width), jnp.float32)],
        cost_estimate=pl.CostEstimate(flops=rows * width * 8, bytes_accessed=2 << 20, transcendentals=rows),
    )(where, pair_index, resid, gain, score, *pieces)


def together(*values):
    return lax.optimization_barrier(values)


def body(
    rank_query,
    rank_key,
    rank_value,
    rank_resid,
    out_weight,
    rank_gain,
    score_weight,
    pair_index,
    cand_rank,
    cand_len,
    blend_owner,
    blend_rows,
    blend_gain,
    blend_weight,
):
    local_heads = HR // NZ
    length = rank_query.shape[1]
    my_y, my_x, my_core, my_z = (lax.axis_index(a) for a in ("y", "x", "core", "z"))

    where = jnp.stack([my_y, my_x, my_core, my_z]).astype(jnp.int32)
    columns = lax.all_gather(out_weight.T, ("x", "core"), axis=0, tiled=True)

    outgoing = select_rows(blend_owner, cand_rank, cand_len, blend_rows)
    rank_query, blend_weight, outgoing = together(rank_query, blend_weight, outgoing)
    prompts = blend_rows.shape[0]
    features = blend_rows.shape[3]
    arrived = lax.all_to_all(
        outgoing.reshape(prompts, -1, features), PLANE, split_axis=0, concat_axis=0, tiled=True
    )
    own = arrived.reshape(prompts * arrived.shape[1], features)

    context = pair_attention(rank_query, rank_key, rank_value, local_heads)
    context = context.reshape(rank_query.shape[0], length, -1)
    half_pairs = context.shape[0] // 2
    c_before = lax.ppermute(context, "y", ring(NY, 1))
    c_after = lax.ppermute(context, "y", ring(NY, -1))
    depth = blend_weight.shape[0]
    slab = (my_y * NX + my_x) * NC + my_core
    gain = lax.dynamic_slice_in_dim(blend_gain, slab * depth, depth, 0).astype(jnp.float32)
    own_slab = (blend_weight.transpose(1, 0, 2).astype(jnp.float32) * gain[None, :, None]).astype(
        jnp.bfloat16
    )[None]
    gain_row = rank_gain.reshape(1, -1)
    score_row = score_weight.reshape(1, -1)
    own, context, c_before, c_after, own_slab, gain_row, score_row, where = together(
        own, context, c_before, c_after, own_slab, gain_row, score_row, where
    )

    lower = lax.ppermute(own, "z", ring(NZ, 1))
    upper = lax.ppermute(own, "z", ring(NZ, -1))
    c_low = lax.ppermute(c_before[:half_pairs], "y", ring(NY, 1))
    c_high = lax.ppermute(c_after[half_pairs:], "y", ring(NY, -1))
    x_before = lax.ppermute(own_slab, "x", ring(NX, 1))
    x_after = lax.ppermute(own_slab, "x", ring(NX, -1))
    x_across = lax.ppermute(x_before, "x", ring(NX, 1))
    strip = jnp.concatenate([own_slab, x_before, x_across, x_after], axis=0)
    lower, upper, strip, context, c_low, c_high = together(
        lower, upper, strip, context, c_low, c_high
    )
    blocks = {1: upper, NZ - 1: lower, 0: own}
    term_rows, token = project([context, c_before, c_low, c_high, c_after], columns)
    part_sum = lax.psum_scatter(
        term_rows.reshape(-1, term_rows.shape[-1]), "z", scatter_dimension=0, tiled=True
    )

    lower = lax.ppermute(lower, "z", ring(NZ, 1))
    upper = lax.ppermute(upper, "z", ring(NZ, -1))
    y_before = lax.ppermute(strip, "y", ring(NY, 1))
    y_after = lax.ppermute(strip, "y", ring(NY, -1))
    lower, upper, token = together(lower, upper, token)
    blocks.update({2: upper, NZ - 2: lower})

    lower = lax.ppermute(lower, "z", ring(NZ, 1))
    upper = lax.ppermute(upper, "z", ring(NZ, -1))
    y_across = jnp.concatenate(
        [
            lax.ppermute(y_before[:2], "y", ring(NY, 1)),
            lax.ppermute(y_after[2:], "y", ring(NY, -1)),
        ],
        axis=0,
    )
    swapped = [lax.ppermute(s, "core", ring(NC, 1)) for s in (strip, y_before, y_after)]
    lower, upper, part_sum, y_across = together(lower, upper, part_sum, y_across)

    swapped.insert(2, lax.ppermute(y_across, "core", ring(NC, 1)))
    slabs = [strip, y_before, y_across, y_after]
    half = own.shape[0] // 2
    low = lax.ppermute(lower[:half], "z", ring(NZ, 1))
    high = lax.ppermute(upper[half:], "z", ring(NZ, -1))
    own_pairs = rank_resid.shape[0]
    parts = part_sum.reshape(NY, own_pairs * length, -1)
    pieces = [lax.ppermute(parts[r], "y", ring(NY, -r)) for r in range(1, NY)]
    weights = arrange(where, token, slabs + swapped)
    near = (0, 1, 2, NZ - 2, NZ - 1)
    total, squares = encode_first(near, [blocks[i] for i in near], weights)
    low, high, squares, *pieces = together(low, high, squares, *pieces)
    pieces = [parts[0]] + pieces

    rank_hidden, votes = norm_and_vote(
        where,
        pair_index,
        rank_resid.reshape(own_pairs * length, -1),
        gain_row,
        score_row,
        pieces,
        prompts,
        cand_rank.shape[1],
    )
    rank_hidden = rank_hidden.reshape(rank_resid.shape)
    for bit in (1, 2, 4):
        votes = votes + lax.ppermute(votes, "z", [(i, i ^ bit) for i in range(NZ)])
    cand_score = votes.T
    blended_qkv = encode_last(
        (3, NZ - 3, 4), upper, lower, low, high, weights, total, squares, prompts
    )
    return (rank_hidden, cand_score, blended_qkv)


def solution(mesh):
    grid = Mesh(mesh.devices.reshape(NY, NX, NC, NZ), ("y", "x", "core", "z"))
    whole = ("y", "x", "core", "z")
    placed = (
        P(PLANE, None, "z"),
        P(PLANE, None, "z"),
        P(PLANE, None, "z"),
        P(whole, None, None),
        P("z", PLANE),
        P(),
        P(),
        P(whole, None),
        P(PLANE, None),
        P(PLANE, None),
        P(PLANE, None),
        P(PLANE, None, None, "z"),
        P(),
        P(PLANE, None, "z"),
    )
    return jax.shard_map(
        body,
        mesh=grid,
        in_specs=placed,
        out_specs=(P(whole, None, None), P(PLANE, None), P(PLANE, None, None, "z")),
        check_vma=False,
    )
```

```python
import math

import jax
import jax.numpy as jnp
from jax import lax
from jax.experimental import pallas as pl
from jax.experimental.pallas import tpu as pltpu
from jax.sharding import Mesh, PartitionSpec as P

HR = 40
HDR = 128
NY, NX, NC, NZ = 4, 4, 2, 8
PLANE = ("y", "x", "core")


def ring(count, step):
    return [(i, (i + step) % count) for i in range(count)]


def pair_attention(queries, keys_in, values_in, head_count):
    pair_count, length, row_width = queries.shape
    head_size = row_width // head_count
    query_heads = queries.reshape(pair_count, length, head_count, head_size)
    key_heads = keys_in.reshape(pair_count, length, head_count, head_size)
    value_heads = values_in.reshape(pair_count, length, head_count, head_size)
    scores = jnp.einsum(
        "pihd,pjhd->phij", query_heads, key_heads, preferred_element_type=jnp.float32
    ) * (1.0 / math.sqrt(HDR))
    highest = jnp.max(scores, axis=-1, keepdims=True)
    weights = jnp.exp(scores - highest)
    soft_weights = (weights / jnp.sum(weights, axis=-1, keepdims=True)).astype(jnp.bfloat16)
    context = jnp.einsum(
        "phij,pjhd->pihd", soft_weights, value_heads, preferred_element_type=jnp.float32
    )
    return context.astype(jnp.bfloat16).reshape(pair_count * length, row_width)


def select_kernel(owner_ref, rank_ref, len_ref, rows_ref, out_ref, cand_ref, live_ref, mask_ref):
    places = rank_ref.shape[0]
    position = lax.broadcasted_iota(jnp.int32, rows_ref.shape[1:], 0)
    for live in range(mask_ref.shape[0]):
        mask_ref[live] = jnp.where(position < live, 1.0, 0.0).astype(mask_ref.dtype)

    def one_prompt(prompt, carry):
        owner = owner_ref[0, prompt]
        for place in range(places):
            rank = rank_ref[place, prompt]
            cand_ref[prompt, rank] = place
            live_ref[prompt, rank] = len_ref[place, prompt]
        for rank in range(3):
            picked = rows_ref[prompt * places + cand_ref[prompt, rank]]
            out_ref[owner * 3 + rank] = picked * mask_ref[live_ref[prompt, rank]]
        return carry

    lax.fori_loop(0, owner_ref.shape[1], one_prompt, 0, unroll=4)


def select_rows(blend_owner, cand_rank, cand_len, blend_rows):
    prompts, cands, length, features = blend_rows.shape
    smem = pl.BlockSpec(memory_space=pltpu.SMEM)
    vmem = pl.BlockSpec(memory_space=pltpu.VMEM)
    return pl.pallas_call(
        select_kernel,
        out_shape=jax.ShapeDtypeStruct((prompts * 3, length, features), blend_rows.dtype),
        in_specs=[smem, smem, smem, vmem],
        out_specs=vmem,
        scratch_shapes=[pltpu.SMEM((prompts, cands), jnp.int32)] * 2
        + [pltpu.VMEM((length + 1, length, features), blend_rows.dtype)],
        cost_estimate=pl.CostEstimate(flops=0, bytes_accessed=3 << 20, transcendentals=0),
    )(blend_owner, cand_rank.T, cand_len.T, blend_rows.reshape(prompts * cands, length, features))


def arrange_kernel(where_ref, token_ref, *refs):
    slab_refs, out_ref = refs[:-1], refs[-1]
    third, depth = slab_refs[0].shape[1:3]
    my_y, my_x, my_core, my_z = where_ref[0], where_ref[1], where_ref[2], where_ref[3]
    for swapped in range(NC):
        for back in range(NY):
            slabs = slab_refs[swapped * NY + back]
            for left in range(NX):
                slab_y = lax.rem(my_y - back + NY, NY)
                slab_x = lax.rem(my_x - left + NX, NX)
                slab_core = lax.rem(my_core + swapped, NC)
                slab = (slab_y * NX + slab_x) * NC + slab_core
                order = lax.rem(slab // 4 - my_z + NZ, NZ)
                start = pl.multiple_of((order * 4 + lax.rem(slab, 4)) * depth, depth)
                for part in range(third):
                    out_ref[part, pl.ds(start, depth), :] = slabs[left, part]


def arrange(where, token, slabs):
    third, depth, width = slabs[0].shape[1:]
    vmem = pl.BlockSpec(memory_space=pltpu.VMEM)
    return pl.pallas_call(
        arrange_kernel,
        out_shape=jax.ShapeDtypeStruct((third, NC * NY * NX * depth, width), jnp.bfloat16),
        in_specs=[pl.BlockSpec(memory_space=pltpu.SMEM)] + [vmem] * (len(slabs) + 1),
        out_specs=vmem,
        compiler_params=pltpu.CompilerParams(vmem_limit_bytes=32 << 20),
        cost_estimate=pl.CostEstimate(flops=0, bytes_accessed=12 << 20, transcendentals=0),
    )(where, token, *slabs)


def project_kernel(rows_ref, columns_ref, out_ref, token_ref):
    token_ref[...] = jnp.zeros_like(token_ref)
    out_ref[...] = lax.dot_general(
        rows_ref[...], columns_ref[...], (((1,), (1,)), ((), ())), preferred_element_type=jnp.float32
    ).astype(out_ref.dtype)


def project(rows, columns):
    count, depth = rows.shape
    width = columns.shape[0]
    steps = 4
    return pl.pallas_call(
        project_kernel,
        out_shape=(
            jax.ShapeDtypeStruct((count, width), jnp.bfloat16),
            jax.ShapeDtypeStruct((8, 128), jnp.float32),
        ),
        grid=(steps,),
        in_specs=[
            pl.BlockSpec((count, depth), lambda i: (0, 0)),
            pl.BlockSpec((width // steps, depth), lambda i: (i, 0)),
        ],
        out_specs=(
            pl.BlockSpec((count, width // steps), lambda i: (0, i)),
            pl.BlockSpec((8, 128), lambda i: (0, 0)),
        ),
        compiler_params=pltpu.CompilerParams(vmem_limit_bytes=16 << 20),
        cost_estimate=pl.CostEstimate(
            flops=2 * count * width * depth, bytes_accessed=9 << 20, transcendentals=0
        ),
    )(rows, columns)


def squares_of(values):
    value = values.astype(jnp.float32)
    return jnp.sum(value * value, axis=-1, keepdims=True)


def first_kernel(orders, *refs):
    row_refs = refs[: len(orders)]
    weight_ref, total_ref, squares_ref = refs[len(orders) :]
    features = row_refs[0].shape[1]
    squares = sum(squares_of(rows[...]) for rows in row_refs)
    squares_ref[...] = jnp.broadcast_to(squares, squares_ref.shape)
    for part in range(weight_ref.shape[0]):
        total_ref[part] = sum(
            jnp.dot(
                rows[...],
                weight_ref[part, order * features : (order + 1) * features, :],
                preferred_element_type=jnp.float32,
            )
            for order, rows in zip(orders, row_refs)
        )


def last_kernel(orders, row_a, row_b, low_ref, high_ref, weight_ref, total_ref, squares_ref, out_ref):
    features = row_a.shape[1]
    half_steps = pl.num_programs(0) // 2
    across = jnp.where(pl.program_id(0) < half_steps, low_ref[...], high_ref[...])
    values = [row_a[...], row_b[...], across]
    squares = squares_ref[:, :1] + sum(squares_of(value) for value in values)
    scale = lax.rsqrt(squares * (1.0 / (NZ * features)) + 1e-06)
    prompts, third, length, width = out_ref.shape
    for part in range(third):
        total = total_ref[part] + sum(
            jnp.dot(
                value,
                weight_ref[part, order * features : (order + 1) * features, :],
                preferred_element_type=jnp.float32,
            )
            for order, value in zip(orders, values)
        )
        out_ref[:, part] = (total * scale).astype(out_ref.dtype).reshape(prompts, length, width)


def whole_spec(array):
    return pl.BlockSpec(array.shape, lambda i: (0,) * array.ndim, pipeline_mode=pl.Buffered(1))


def encode_first(orders, blocks, weights):
    rows, features = blocks[0].shape
    third, _, width = weights.shape
    steps = 4
    step_rows = rows // steps
    return pl.pallas_call(
        lambda *refs: first_kernel(orders, *refs),
        out_shape=(
            jax.ShapeDtypeStruct((third, rows, width), jnp.float32),
            jax.ShapeDtypeStruct((rows, 128), jnp.float32),
        ),
        grid=(steps,),
        in_specs=[pl.BlockSpec((step_rows, features), lambda i: (i, 0))] * len(blocks)
        + [whole_spec(weights)],
        out_specs=(
            pl.BlockSpec((third, step_rows, width), lambda i: (0, i, 0)),
            pl.BlockSpec((step_rows, 128), lambda i: (i, 0)),
        ),
        compiler_params=pltpu.CompilerParams(vmem_limit_bytes=24 << 20),
        cost_estimate=pl.CostEstimate(
            flops=2 * rows * len(blocks) * features * third * width,
            bytes_accessed=12 << 20,
            transcendentals=0,
        ),
    )(*blocks, weights)


def encode_last(orders, row_a, row_b, low, high, weights, total, squares, prompts):
    rows, features = row_a.shape
    third, _, width = weights.shape
    length = rows // prompts
    steps = 4
    step_rows = rows // steps
    step_prompts = prompts // steps
    out = pl.pallas_call(
        lambda *refs: last_kernel(orders, *refs),
        out_shape=jax.ShapeDtypeStruct((prompts, third, length, width), jnp.bfloat16),
        grid=(steps,),
        in_specs=[
            pl.BlockSpec((step_rows, features), lambda i: (i, 0)),
            pl.BlockSpec((step_rows, features), lambda i: (i, 0)),
            pl.BlockSpec((step_rows, features), lambda i: (jnp.minimum(i, steps // 2 - 1), 0)),
            pl.BlockSpec((step_rows, features), lambda i: (jnp.maximum(i - steps // 2, 0), 0)),
            whole_spec(weights),
            pl.BlockSpec((third, step_rows, width), lambda i: (0, i, 0)),
            pl.BlockSpec((step_rows, 128), lambda i: (i, 0)),
        ],
        out_specs=pl.BlockSpec((step_prompts, third, length, width), lambda i: (i, 0, 0, 0)),
        compiler_params=pltpu.CompilerParams(vmem_limit_bytes=24 << 20),
        cost_estimate=pl.CostEstimate(
            flops=36 * rows * 3 * features * third * width,
            bytes_accessed=12 << 20,
            transcendentals=rows,
        ),
    )(row_a, row_b, low, high, weights, total, squares)
    return out.transpose(0, 2, 1, 3)


def norm_kernel(pair_ref, resid_ref, gain_ref, score_ref, sum_ref, hidden_ref, votes_ref):
    mixed = resid_ref[...].astype(jnp.float32) + sum_ref[...].astype(jnp.float32)
    squares = jnp.sum(mixed * mixed, axis=-1, keepdims=True)
    scale = lax.rsqrt(squares * (1.0 / mixed.shape[1]) + 1e-05)
    normed = mixed * scale * gain_ref[...].astype(jnp.float32)
    hidden_ref[...] = normed.astype(hidden_ref.dtype)
    logit = jnp.sum(normed[:1] * score_ref[...].astype(jnp.float32), axis=-1, keepdims=True)
    cand = lax.broadcasted_iota(jnp.int32, votes_ref.shape, 0)
    prompt = lax.broadcasted_iota(jnp.int32, votes_ref.shape, 1)
    own = prompt == pair_ref[0, 0]
    upward = jnp.where(own & (cand == pair_ref[0, 1]), logit, 0.0)
    downward = jnp.where(own & (cand == pair_ref[0, 2]), logit, 0.0)
    votes_ref[...] = upward - downward


def norm_and_vote(pair_index, resid, gain, score, part_sum, prompts, cands):
    rows, width = resid.shape
    vmem = pl.BlockSpec(memory_space=pltpu.VMEM)
    return pl.pallas_call(
        norm_kernel,
        out_shape=(
            jax.ShapeDtypeStruct((rows, width), jnp.bfloat16),
            jax.ShapeDtypeStruct((cands, prompts), jnp.float32),
        ),
        in_specs=[pl.BlockSpec(memory_space=pltpu.SMEM)] + [vmem] * 4,
        out_specs=(vmem, vmem),
        cost_estimate=pl.CostEstimate(
            flops=rows * width * 8, bytes_accessed=2 << 20, transcendentals=rows
        ),
    )(pair_index, resid, gain, score, part_sum)


def together(*values):
    return lax.optimization_barrier(values)


def body(
    rank_query,
    rank_key,
    rank_value,
    rank_resid,
    out_weight,
    rank_gain,
    score_weight,
    pair_index,
    cand_rank,
    cand_len,
    blend_owner,
    blend_rows,
    blend_gain,
    blend_weight,
):
    local_heads = HR // NZ
    length = rank_query.shape[1]
    my_y, my_x, my_core, my_z = (lax.axis_index(a) for a in ("y", "x", "core", "z"))

    where = jnp.stack([my_y, my_x, my_core, my_z]).astype(jnp.int32)
    columns = lax.all_gather(out_weight.T, PLANE, axis=0, tiled=True)

    outgoing = select_rows(blend_owner, cand_rank, cand_len, blend_rows)
    rank_query, blend_weight, outgoing = together(rank_query, blend_weight, outgoing)
    prompts = blend_rows.shape[0]
    features = blend_rows.shape[3]
    arrived = lax.all_to_all(
        outgoing.reshape(prompts, -1, features), PLANE, split_axis=0, concat_axis=0, tiled=True
    )
    own = arrived.reshape(prompts * arrived.shape[1], features)

    context = pair_attention(rank_query, rank_key, rank_value, local_heads)
    depth = blend_weight.shape[0]
    slab = (my_y * NX + my_x) * NC + my_core
    gain = lax.dynamic_slice_in_dim(blend_gain, slab * depth, depth, 0).astype(jnp.float32)
    own_slab = (blend_weight.transpose(1, 0, 2).astype(jnp.float32) * gain[None, :, None]).astype(
        jnp.bfloat16
    )[None]
    gain_row = rank_gain.reshape(1, -1)
    score_row = score_weight.reshape(1, -1)
    own, context, own_slab, gain_row, score_row, where = together(
        own, context, own_slab, gain_row, score_row, where
    )

    lower = lax.ppermute(own, "z", ring(NZ, 1))
    upper = lax.ppermute(own, "z", ring(NZ, -1))
    x_before = lax.ppermute(own_slab, "x", ring(NX, 1))
    x_after = lax.ppermute(own_slab, "x", ring(NX, -1))
    x_across = lax.ppermute(x_before, "x", ring(NX, 1))
    strip = jnp.concatenate([own_slab, x_before, x_across, x_after], axis=0)
    lower, upper, strip, context = together(lower, upper, strip, context)
    blocks = {1: upper, NZ - 1: lower, 0: own}

    lower = lax.ppermute(lower, "z", ring(NZ, 1))
    upper = lax.ppermute(upper, "z", ring(NZ, -1))
    y_before = lax.ppermute(strip, "y", ring(NY, 1))
    y_after = lax.ppermute(strip, "y", ring(NY, -1))
    term_rows, token = project(context, columns)
    lower, upper, token = together(lower, upper, token)
    blocks.update({2: upper, NZ - 2: lower})
    part_sum = lax.psum_scatter(term_rows, "z", scatter_dimension=0, tiled=True)

    lower = lax.ppermute(lower, "z", ring(NZ, 1))
    upper = lax.ppermute(upper, "z", ring(NZ, -1))
    y_across = jnp.concatenate(
        [
            lax.ppermute(y_before[:2], "y", ring(NY, 1)),
            lax.ppermute(y_after[2:], "y", ring(NY, -1)),
        ],
        axis=0,
    )
    lower, upper, y_across = together(lower, upper, y_across)

    slabs = [strip, y_before, y_across, y_after]
    weights = arrange(where, token, slabs + [lax.ppermute(s, "core", ring(NC, 1)) for s in slabs])
    near = (0, 1, 2, NZ - 2, NZ - 1)
    half = own.shape[0] // 2
    total, squares = encode_first(near, [blocks[i] for i in near], weights)
    low = lax.ppermute(lower[:half], "z", ring(NZ, 1))
    high = lax.ppermute(upper[half:], "z", ring(NZ, -1))
    blended_qkv = encode_last(
        (3, NZ - 3, 4), upper, lower, low, high, weights, total, squares, prompts
    )

    part_sum, blended_qkv = together(part_sum, blended_qkv)
    own_pairs = rank_resid.shape[0]
    rank_hidden, votes = norm_and_vote(
        pair_index,
        rank_resid.reshape(own_pairs * length, -1),
        gain_row,
        score_row,
        part_sum,
        prompts,
        cand_rank.shape[1],
    )
    rank_hidden = rank_hidden.reshape(rank_resid.shape)
    votes = jnp.broadcast_to(votes[None], (NZ,) + votes.shape)
    votes = lax.all_to_all(votes, "z", split_axis=0, concat_axis=0, tiled=True)
    cand_score = jnp.sum(votes, axis=0).T
    return (rank_hidden, cand_score, blended_qkv)


def solution(mesh):
    grid = Mesh(mesh.devices.reshape(NY, NX, NC, NZ), ("y", "x", "core", "z"))
    whole = ("y", "x", "core", "z")
    placed = (
        P(PLANE, None, "z"),
        P(PLANE, None, "z"),
        P(PLANE, None, "z"),
        P(whole, None, None),
        P("z", PLANE),
        P(),
        P(),
        P(whole, None),
        P(PLANE, None),
        P(PLANE, None),
        P(PLANE, None),
        P(PLANE, None, None, "z"),
        P(),
        P(PLANE, None, "z"),
    )
    return jax.shard_map(
        body,
        mesh=grid,
        in_specs=placed,
        out_specs=(P(whole, None, None), P(PLANE, None), P(PLANE, None, None, "z")),
        check_vma=False,
    )
```

```python
import math

import jax
import jax.numpy as jnp
from jax import lax
from jax.experimental import pallas as pl
from jax.experimental.pallas import tpu as pltpu
from jax.sharding import Mesh, PartitionSpec as P

HR = 40
HDR = 128
NY, NX, NC, NZ = 4, 4, 2, 8
PLANE = ("y", "x", "core")


def ring(count, step):
    return [(i, (i + step) % count) for i in range(count)]


def pair_attention(queries, keys_in, values_in, head_count):
    pair_count, length, row_width = queries.shape
    head_size = row_width // head_count
    query_heads = queries.reshape(pair_count, length, head_count, head_size)
    key_heads = keys_in.reshape(pair_count, length, head_count, head_size)
    value_heads = values_in.reshape(pair_count, length, head_count, head_size)
    scores = jnp.einsum(
        "pihd,pjhd->phij", query_heads, key_heads, preferred_element_type=jnp.float32
    ) * (1.0 / math.sqrt(HDR))
    highest = jnp.max(scores, axis=-1, keepdims=True)
    weights = jnp.exp(scores - highest)
    soft_weights = (weights / jnp.sum(weights, axis=-1, keepdims=True)).astype(jnp.bfloat16)
    context = jnp.einsum(
        "phij,pjhd->pihd", soft_weights, value_heads, preferred_element_type=jnp.float32
    )
    return context.astype(jnp.bfloat16).reshape(pair_count * length, row_width)


def select_kernel(owner_ref, rank_ref, len_ref, rows_ref, out_ref, cand_ref, live_ref, mask_ref):
    places = rank_ref.shape[0]
    position = lax.broadcasted_iota(jnp.int32, rows_ref.shape[1:], 0)
    for live in range(mask_ref.shape[0]):
        mask_ref[live] = jnp.where(position < live, 1.0, 0.0).astype(mask_ref.dtype)

    def one_prompt(prompt, carry):
        owner = owner_ref[0, prompt]
        for place in range(places):
            rank = rank_ref[place, prompt]
            cand_ref[prompt, rank] = place
            live_ref[prompt, rank] = len_ref[place, prompt]
        for rank in range(3):
            picked = rows_ref[prompt * places + cand_ref[prompt, rank]]
            out_ref[owner * 3 + rank] = picked * mask_ref[live_ref[prompt, rank]]
        return carry

    lax.fori_loop(0, owner_ref.shape[1], one_prompt, 0, unroll=4)


def select_rows(blend_owner, cand_rank, cand_len, blend_rows):
    prompts, cands, length, features = blend_rows.shape
    smem = pl.BlockSpec(memory_space=pltpu.SMEM)
    vmem = pl.BlockSpec(memory_space=pltpu.VMEM)
    return pl.pallas_call(
        select_kernel,
        out_shape=jax.ShapeDtypeStruct((prompts * 3, length, features), blend_rows.dtype),
        in_specs=[smem, smem, smem, vmem],
        out_specs=vmem,
        scratch_shapes=[pltpu.SMEM((prompts, cands), jnp.int32)] * 2
        + [pltpu.VMEM((length + 1, length, features), blend_rows.dtype)],
        cost_estimate=pl.CostEstimate(flops=0, bytes_accessed=3 << 20, transcendentals=0),
    )(blend_owner, cand_rank.T, cand_len.T, blend_rows.reshape(prompts * cands, length, features))


def arrange_kernel(where_ref, token_ref, *refs):
    slab_refs, out_ref = refs[:-1], refs[-1]
    third, depth = slab_refs[0].shape[1:3]
    my_y, my_x, my_core, my_z = where_ref[0], where_ref[1], where_ref[2], where_ref[3]
    for swapped in range(NC):
        for back in range(NY):
            slabs = slab_refs[swapped * NY + back]
            for left in range(NX):
                slab_y = lax.rem(my_y - back + NY, NY)
                slab_x = lax.rem(my_x - left + NX, NX)
                slab_core = lax.rem(my_core + swapped, NC)
                slab = (slab_y * NX + slab_x) * NC + slab_core
                order = lax.rem(slab // 4 - my_z + NZ, NZ)
                start = pl.multiple_of((order * 4 + lax.rem(slab, 4)) * depth, depth)
                for part in range(third):
                    out_ref[part, pl.ds(start, depth), :] = slabs[left, part]


def arrange(where, token, slabs):
    third, depth, width = slabs[0].shape[1:]
    vmem = pl.BlockSpec(memory_space=pltpu.VMEM)
    return pl.pallas_call(
        arrange_kernel,
        out_shape=jax.ShapeDtypeStruct((third, NC * NY * NX * depth, width), jnp.bfloat16),
        in_specs=[pl.BlockSpec(memory_space=pltpu.SMEM)] + [vmem] * (len(slabs) + 1),
        out_specs=vmem,
        compiler_params=pltpu.CompilerParams(vmem_limit_bytes=32 << 20),
        cost_estimate=pl.CostEstimate(flops=0, bytes_accessed=12 << 20, transcendentals=0),
    )(where, token, *slabs)


def project_kernel(rows_ref, columns_ref, out_ref, token_ref):
    token_ref[...] = jnp.zeros_like(token_ref)
    out_ref[...] = lax.dot_general(
        rows_ref[...], columns_ref[...], (((1,), (1,)), ((), ())), preferred_element_type=jnp.float32
    ).astype(out_ref.dtype)


def project(rows, columns):
    count, depth = rows.shape
    width = columns.shape[0]
    steps = 4
    return pl.pallas_call(
        project_kernel,
        out_shape=(
            jax.ShapeDtypeStruct((count, width), jnp.bfloat16),
            jax.ShapeDtypeStruct((8, 128), jnp.float32),
        ),
        grid=(steps,),
        in_specs=[
            pl.BlockSpec((count, depth), lambda i: (0, 0)),
            pl.BlockSpec((width // steps, depth), lambda i: (i, 0)),
        ],
        out_specs=(
            pl.BlockSpec((count, width // steps), lambda i: (0, i)),
            pl.BlockSpec((8, 128), lambda i: (0, 0)),
        ),
        compiler_params=pltpu.CompilerParams(vmem_limit_bytes=56 << 20),
        cost_estimate=pl.CostEstimate(
            flops=2 * count * width * depth, bytes_accessed=9 << 20, transcendentals=0
        ),
    )(rows, columns)


def squares_of(values):
    value = values.astype(jnp.float32)
    return jnp.sum(value * value, axis=-1, keepdims=True)


def first_kernel(orders, *refs):
    row_refs = refs[: len(orders)]
    weight_ref, total_ref, squares_ref = refs[len(orders) :]
    features = row_refs[0].shape[1]
    squares = sum(squares_of(rows[...]) for rows in row_refs)
    squares_ref[...] = jnp.broadcast_to(squares, squares_ref.shape)
    for part in range(weight_ref.shape[0]):
        total_ref[part] = sum(
            jnp.dot(
                rows[...],
                weight_ref[part, order * features : (order + 1) * features, :],
                preferred_element_type=jnp.float32,
            )
            for order, rows in zip(orders, row_refs)
        )


def last_kernel(orders, row_a, row_b, low_ref, high_ref, weight_ref, total_ref, squares_ref, out_ref):
    features = row_a.shape[1]
    half_steps = pl.num_programs(0) // 2
    across = jnp.where(pl.program_id(0) < half_steps, low_ref[...], high_ref[...])
    values = [row_a[...], row_b[...], across]
    squares = squares_ref[:, :1] + sum(squares_of(value) for value in values)
    scale = lax.rsqrt(squares * (1.0 / (NZ * features)) + 1e-06)
    prompts, third, length, width = out_ref.shape
    for part in range(third):
        total = total_ref[part] + sum(
            jnp.dot(
                value,
                weight_ref[part, order * features : (order + 1) * features, :],
                preferred_element_type=jnp.float32,
            )
            for order, value in zip(orders, values)
        )
        out_ref[:, part] = (total * scale).astype(out_ref.dtype).reshape(prompts, length, width)


def whole_spec(array):
    return pl.BlockSpec(array.shape, lambda i: (0,) * array.ndim, pipeline_mode=pl.Buffered(1))


def encode_first(orders, blocks, weights):
    rows, features = blocks[0].shape
    third, _, width = weights.shape
    steps = 4
    step_rows = rows // steps
    return pl.pallas_call(
        lambda *refs: first_kernel(orders, *refs),
        out_shape=(
            jax.ShapeDtypeStruct((third, rows, width), jnp.float32),
            jax.ShapeDtypeStruct((rows, 128), jnp.float32),
        ),
        grid=(steps,),
        in_specs=[pl.BlockSpec((step_rows, features), lambda i: (i, 0))] * len(blocks)
        + [whole_spec(weights)],
        out_specs=(
            pl.BlockSpec((third, step_rows, width), lambda i: (0, i, 0)),
            pl.BlockSpec((step_rows, 128), lambda i: (i, 0)),
        ),
        compiler_params=pltpu.CompilerParams(vmem_limit_bytes=24 << 20),
        cost_estimate=pl.CostEstimate(
            flops=2 * rows * len(blocks) * features * third * width,
            bytes_accessed=12 << 20,
            transcendentals=0,
        ),
    )(*blocks, weights)


def encode_last(orders, row_a, row_b, low, high, weights, total, squares, prompts):
    rows, features = row_a.shape
    third, _, width = weights.shape
    length = rows // prompts
    steps = 4
    step_rows = rows // steps
    step_prompts = prompts // steps
    out = pl.pallas_call(
        lambda *refs: last_kernel(orders, *refs),
        out_shape=jax.ShapeDtypeStruct((prompts, third, length, width), jnp.bfloat16),
        grid=(steps,),
        in_specs=[
            pl.BlockSpec((step_rows, features), lambda i: (i, 0)),
            pl.BlockSpec((step_rows, features), lambda i: (i, 0)),
            pl.BlockSpec((step_rows, features), lambda i: (jnp.minimum(i, steps // 2 - 1), 0)),
            pl.BlockSpec((step_rows, features), lambda i: (jnp.maximum(i - steps // 2, 0), 0)),
            whole_spec(weights),
            pl.BlockSpec((third, step_rows, width), lambda i: (0, i, 0)),
            pl.BlockSpec((step_rows, 128), lambda i: (i, 0)),
        ],
        out_specs=pl.BlockSpec((step_prompts, third, length, width), lambda i: (i, 0, 0, 0)),
        compiler_params=pltpu.CompilerParams(vmem_limit_bytes=24 << 20),
        cost_estimate=pl.CostEstimate(
            flops=36 * rows * 3 * features * third * width,
            bytes_accessed=12 << 20,
            transcendentals=rows,
        ),
    )(row_a, row_b, low, high, weights, total, squares)
    return out.transpose(0, 2, 1, 3)


def norm_kernel(pair_ref, resid_ref, gain_ref, score_ref, sum_ref, hidden_ref, votes_ref):
    mixed = resid_ref[...].astype(jnp.float32) + sum_ref[...].astype(jnp.float32)
    squares = jnp.sum(mixed * mixed, axis=-1, keepdims=True)
    scale = lax.rsqrt(squares * (1.0 / mixed.shape[1]) + 1e-05)
    normed = mixed * scale * gain_ref[...].astype(jnp.float32)
    hidden_ref[...] = normed.astype(hidden_ref.dtype)
    logit = jnp.sum(normed[:1] * score_ref[...].astype(jnp.float32), axis=-1, keepdims=True)
    cand = lax.broadcasted_iota(jnp.int32, votes_ref.shape, 0)
    prompt = lax.broadcasted_iota(jnp.int32, votes_ref.shape, 1)
    own = prompt == pair_ref[0, 0]
    upward = jnp.where(own & (cand == pair_ref[0, 1]), logit, 0.0)
    downward = jnp.where(own & (cand == pair_ref[0, 2]), logit, 0.0)
    votes_ref[...] = upward - downward


def norm_and_vote(pair_index, resid, gain, score, part_sum, prompts, cands):
    rows, width = resid.shape
    vmem = pl.BlockSpec(memory_space=pltpu.VMEM)
    return pl.pallas_call(
        norm_kernel,
        out_shape=(
            jax.ShapeDtypeStruct((rows, width), jnp.bfloat16),
            jax.ShapeDtypeStruct((cands, prompts), jnp.float32),
        ),
        in_specs=[pl.BlockSpec(memory_space=pltpu.SMEM)] + [vmem] * 4,
        out_specs=(vmem, vmem),
        cost_estimate=pl.CostEstimate(
            flops=rows * width * 8, bytes_accessed=2 << 20, transcendentals=rows
        ),
    )(pair_index, resid, gain, score, part_sum)


def together(*values):
    return lax.optimization_barrier(values)


def body(
    rank_query,
    rank_key,
    rank_value,
    rank_resid,
    out_weight,
    rank_gain,
    score_weight,
    pair_index,
    cand_rank,
    cand_len,
    blend_owner,
    blend_rows,
    blend_gain,
    blend_weight,
):
    local_heads = HR // NZ
    length = rank_query.shape[1]
    my_y, my_x, my_core, my_z = (lax.axis_index(a) for a in ("y", "x", "core", "z"))

    where = jnp.stack([my_y, my_x, my_core, my_z]).astype(jnp.int32)
    columns = lax.all_gather(out_weight.T, PLANE, axis=0, tiled=True)

    outgoing = select_rows(blend_owner, cand_rank, cand_len, blend_rows)
    rank_query, blend_weight, outgoing = together(rank_query, blend_weight, outgoing)
    prompts = blend_rows.shape[0]
    features = blend_rows.shape[3]
    arrived = lax.all_to_all(
        outgoing.reshape(prompts, -1, features), PLANE, split_axis=0, concat_axis=0, tiled=True
    )
    own = arrived.reshape(prompts * arrived.shape[1], features)

    context = pair_attention(rank_query, rank_key, rank_value, local_heads)
    depth = blend_weight.shape[0]
    slab = (my_y * NX + my_x) * NC + my_core
    gain = lax.dynamic_slice_in_dim(blend_gain, slab * depth, depth, 0).astype(jnp.float32)
    own_slab = (blend_weight.transpose(1, 0, 2).astype(jnp.float32) * gain[None, :, None]).astype(
        jnp.bfloat16
    )[None]
    gain_row = rank_gain.reshape(1, -1)
    score_row = score_weight.reshape(1, -1)
    own, context, own_slab, gain_row, score_row, where = together(
        own, context, own_slab, gain_row, score_row, where
    )

    lower = lax.ppermute(own, "z", ring(NZ, 1))
    upper = lax.ppermute(own, "z", ring(NZ, -1))
    x_before = lax.ppermute(own_slab, "x", ring(NX, 1))
    x_after = lax.ppermute(own_slab, "x", ring(NX, -1))
    x_across = lax.ppermute(x_before, "x", ring(NX, 1))
    strip = jnp.concatenate([own_slab, x_before, x_across, x_after], axis=0)
    lower, upper, strip, context = together(lower, upper, strip, context)
    blocks = {1: upper, NZ - 1: lower, 0: own}

    lower = lax.ppermute(lower, "z", ring(NZ, 1))
    upper = lax.ppermute(upper, "z", ring(NZ, -1))
    y_before = lax.ppermute(strip, "y", ring(NY, 1))
    y_after = lax.ppermute(strip, "y", ring(NY, -1))
    term_rows, token = project(context, columns)
    lower, upper, token = together(lower, upper, token)
    blocks.update({2: upper, NZ - 2: lower})
    part_sum = lax.psum_scatter(term_rows, "z", scatter_dimension=0, tiled=True)

    lower = lax.ppermute(lower, "z", ring(NZ, 1))
    upper = lax.ppermute(upper, "z", ring(NZ, -1))
    y_across = jnp.concatenate(
        [
            lax.ppermute(y_before[:2], "y", ring(NY, 1)),
            lax.ppermute(y_after[2:], "y", ring(NY, -1)),
        ],
        axis=0,
    )
    lower, upper, y_across = together(lower, upper, y_across)

    slabs = [strip, y_before, y_across, y_after]
    weights = arrange(where, token, slabs + [lax.ppermute(s, "core", ring(NC, 1)) for s in slabs])
    near = (0, 1, 2, NZ - 2, NZ - 1)
    half = own.shape[0] // 2
    total, squares = encode_first(near, [blocks[i] for i in near], weights)
    low = lax.ppermute(lower[:half], "z", ring(NZ, 1))
    high = lax.ppermute(upper[half:], "z", ring(NZ, -1))
    blended_qkv = encode_last(
        (3, NZ - 3, 4), upper, lower, low, high, weights, total, squares, prompts
    )

    part_sum, blended_qkv = together(part_sum, blended_qkv)
    own_pairs = rank_resid.shape[0]
    rank_hidden, votes = norm_and_vote(
        pair_index,
        rank_resid.reshape(own_pairs * length, -1),
        gain_row,
        score_row,
        part_sum,
        prompts,
        cand_rank.shape[1],
    )
    rank_hidden = rank_hidden.reshape(rank_resid.shape)
    votes = jnp.broadcast_to(votes[None], (NZ,) + votes.shape)
    votes = lax.all_to_all(votes, "z", split_axis=0, concat_axis=0, tiled=True)
    cand_score = jnp.sum(votes, axis=0).T
    return (rank_hidden, cand_score, blended_qkv)


def solution(mesh):
    grid = Mesh(mesh.devices.reshape(NY, NX, NC, NZ), ("y", "x", "core", "z"))
    whole = ("y", "x", "core", "z")
    placed = (
        P(PLANE, None, "z"),
        P(PLANE, None, "z"),
        P(PLANE, None, "z"),
        P(whole, None, None),
        P("z", PLANE),
        P(),
        P(),
        P(whole, None),
        P(PLANE, None),
        P(PLANE, None),
        P(PLANE, None),
        P(PLANE, None, None, "z"),
        P(),
        P(PLANE, None, "z"),
    )
    return jax.shard_map(
        body,
        mesh=grid,
        in_specs=placed,
        out_specs=(P(whole, None, None), P(PLANE, None), P(PLANE, None, None, "z")),
        check_vma=False,
    )
```
